256 devices in a mesh: sweep: 16 (over x_lo, y, core), span: 16 (over x_hi, z).
Axes of the slice: x: 4 (x_hi: 2, x_lo: 2; x = x_hi * 2 + x_lo), y: 4, z: 8, core: 2. Of those that a mesh axis runs over, the one named last changes fastest.
Arguments:
- right_side: float32 [32, 16, 625, 512], P('sweep', 'span'), may hold values from -6 to 6
- start_field: float32 [32, 16, 625, 512], P('sweep', 'span'), may hold values from -6 to 6
- block_inverse: float32 [32, 16, 625, 625], P('sweep', 'span'), may hold values from -0.25 to 0.25
- upwind_block: float32 [32, 16, 625, 125], P('sweep', 'span'), may hold values from -1 to 1
- south_block: float32 [32, 16, 625, 125], P('sweep', 'span'), may hold values from -0.625 to 0.625
- north_block: float32 [32, 16, 625, 125], P('sweep', 'span'), may hold values from -0.625 to 0.625
Outputs:
- solution: float32 [32, 16, 625, 512], P('sweep', 'span')
The draws below stay inside these ranges and needn't reach their ends.
All inputs are finite; a program needn't handle non-finite values.
Results may differ from the reference program's by a relative error of at most 0.00022.
Values sent between devices are 32-bit elements; how exact they have to be, the bound alone decides.
A program may use at most 128 MiB of HBM per device.

```python
import jax
import jax.numpy as jnp
from jax import lax

VARS = 5
NODE = 5
UNK = 625
FACE = 125
SWEEPS = 2
R = 512
NI = 32
NJ = 16


def block_levels(key, shape, shards, low, top_value):
    gain = 1.0
    for dim, blocks in shards:
        draws = jax.random.uniform(jax.random.fold_in(jax.random.fold_in(key, 6), dim), (blocks,), jnp.float32, low / len(shards), top_value / len(shards))
        gain = gain * jnp.repeat(jnp.exp(draws), shape[dim] // blocks).reshape((-1,) + (1,) * (len(shape) - 1 - dim))
    return gain


def normal_values(stream_key, dims, scale, most, split=(), held_as=jnp.bfloat16):
    gain = block_levels(stream_key, dims, split, -0.22, 0.18) if split else 1.0
    result = jax.random.normal(stream_key, dims, jnp.float32) * scale * gain
    return jnp.minimum(jnp.maximum(result, -most), most).astype(held_as)


def setup_inputs(seed: int = 0) -> dict:
    keys = jax.random.split(jax.random.key(seed), 7)
    right_side = normal_values(keys[0], (NI, NJ, UNK, R), 1.0, 6.0, ((0, 16), (1, 16)), jnp.float32)
    start_field = normal_values(keys[1], (NI, NJ, UNK, R), 1.0, 6.0, ((0, 16), (1, 16)), jnp.float32)
    block_inverse = normal_values(keys[2], (NI, NJ, UNK, UNK), UNK ** -0.5, 0.25, ((0, 16), (1, 16)), jnp.float32)
    upwind_block = normal_values(keys[3], (NI, NJ, UNK, FACE), (0.85 / FACE ** 0.5), 1.0, ((0, 16), (1, 16)), jnp.float32)
    south_block = normal_values(keys[4], (NI, NJ, UNK, FACE), (0.5 / FACE ** 0.5), 0.625, ((0, 16), (1, 16)), jnp.float32)
    north_block = normal_values(keys[5], (NI, NJ, UNK, FACE), (0.5 / FACE ** 0.5), 0.625, ((0, 16), (1, 16)), jnp.float32)
    return dict(right_side=right_side, start_field=start_field, block_inverse=block_inverse, upwind_block=upwind_block, south_block=south_block, north_block=north_block)


def face_grid(field):
    leading = field.shape[:-2]
    return field.reshape(leading + (VARS, NODE, NODE, NODE, field.shape[-1]))


def down_face(field):
    leading = field.shape[:-2]
    return face_grid(field)[..., :, NODE - 1, :, :, :].reshape(leading + (FACE, field.shape[-1]))


def high_face(field):
    leading = field.shape[:-2]
    return face_grid(field)[..., :, :, NODE - 1, :, :].reshape(leading + (FACE, field.shape[-1]))


def low_face(field):
    leading = field.shape[:-2]
    return face_grid(field)[..., :, :, 0, :, :].reshape(leading + (FACE, field.shape[-1]))


def batched_product(matrix, vectors):
    return jnp.einsum("...ab,...br->...ar", matrix, vectors, precision=lax.Precision.HIGHEST)


def reference(right_side, start_field, block_inverse, upwind_block, south_block, north_block):
    field = start_field
    span_count = start_field.shape[1]
    columns = start_field.shape[-1]
    for sweep_no in range(SWEEPS):
        south_traces = jnp.roll(high_face(field), 1, axis=1)
        north_traces = jnp.roll(low_face(field), -1, axis=1)
        forcing = right_side - batched_product(south_block, south_traces) - batched_product(north_block, north_traces)

        def element_row(inflow, row_data):
            forcing_row, inverse_row, upwind_row = row_data
            residual = forcing_row - batched_product(upwind_row, inflow)
            solved = batched_product(inverse_row, residual)
            return down_face(solved), solved

        start_trace = jnp.zeros((span_count, FACE, columns), jnp.float32)
        _, field = lax.scan(element_row, start_trace, (forcing, block_inverse, upwind_block))
    return field
```

```python
import jax
import jax.numpy as jnp
from jax import lax
from jax.experimental import pallas as pl
from jax.experimental.pallas import tpu as pltpu
from jax.sharding import PartitionSpec as P

VARS = 5
NODE = 5
UNK = 625
FACE = 125
F = 128
U = 640
W = 128
NP = 4
NQ = 2 * NP
RING = 4
MESH = pl.DeviceIdType.MESH
f32 = jnp.float32
bf16 = jnp.bfloat16


def dot(a, b):
    return jnp.dot(a, b, preferred_element_type=f32)


def halves(x):
    hi = x.astype(bf16)
    lo = (x - hi.astype(f32)).astype(bf16)
    return hi, lo


def left3(x):
    hi, lo = halves(x)
    return jnp.concatenate([hi, lo, hi], axis=1)


def right3(x):
    hi, lo = halves(x)
    return jnp.concatenate([hi, hi, lo], axis=0)


def product(a, b):
    return dot(left3(a), right3(b))


def kernel(
    faces, b_in, snu_in, f_in,
    out,
    bst, snust, fst, sh, sl, fh, fl, dbst, dfull, bfp, bsn3, bu3, hst, hsn3, hu3, hlf,
    gsn3, dsn3, m3, gf, g0f, phi, phik, coef, ca3, e3, phi3,
    sn, xq, gown, gpar, g0c, g0v, ag, xs, xb, tp, tin, ts, zs, hb, ob,
    load_sem, out_sem, zsend, zrecv, gsend, grecv, asend, arecv, xsend, xrecv, tsend, trecv,
    psend, precv, ksend, krecv,
):
    p = lax.axis_index("sweep")
    j = lax.axis_index("span")
    span = 16
    core = lax.rem(p, 2)
    chip = p // 2
    y = lax.rem(chip, RING)
    x = chip // RING
    mate = p + 1 - 2 * core
    up = lax.rem(j + 1, span)
    down = lax.rem(j + span - 1, span)

    def ring_peer(d):
        return (x * RING + lax.rem(y + d, RING)) * 2 + core

    over = lax.rem(p + 8, 16)

    loads = [
        pltpu.make_async_copy(b_in, bst, load_sem.at[0]),
        pltpu.make_async_copy(snu_in, snust, load_sem.at[1]),
        pltpu.make_async_copy(f_in, fst, load_sem.at[2]),
    ]
    for c in loads:
        c.start()

    barrier = pltpu.get_barrier_semaphore()
    for dev in ({"span": up}, {"span": down}, {"sweep": mate}, {"sweep": over},
                {"sweep": ring_peer(1)}, {"sweep": ring_peer(2)}, {"sweep": ring_peer(3)}):
        pl.semaphore_signal(barrier, inc=1, device_id=dev, device_id_type=MESH)
    pl.semaphore_wait(barrier, 7)

    def remote(src, dst, ss, rs, dev):
        return pltpu.make_async_remote_copy(
            src_ref=src, dst_ref=dst, send_sem=ss, recv_sem=rs, device_id=dev, device_id_type=MESH
        )

    def zdev(way):
        return {"span": up if way == 0 else down}

    def zcopy1(c, way):
        return remote(faces.at[way, c], sn.at[c, way], zsend.at[c, way], zrecv.at[c, way], zdev(way))

    def zcopy2(q, way):
        c = lax.rem(q, NP)
        return remote(zs.at[c, way], sn.at[q, way], zsend.at[q, way], zrecv.at[q, way], zdev(way))

    for c in range(NP):
        for way in range(2):
            zcopy1(c, way).start()

    def gcopy(q):
        return remote(gown.at[q], gpar.at[q], gsend.at[q], grecv.at[q], {"sweep": mate})

    def acopy(q, d):
        return remote(ag.at[q, y], ag.at[q, y], asend.at[q, d - 1], arecv.at[q, y], {"sweep": ring_peer(d)})

    def aland(q, d):
        k = lax.rem(y + RING - d, RING)
        return remote(ag.at[q, k], ag.at[q, k], asend.at[q, d - 1], arecv.at[q, k], {"sweep": ring_peer(d)})

    def xcopy(q):
        return remote(xs.at[q], xb.at[q], xsend.at[q], xrecv.at[q], {"sweep": over})

    def tcopy(q):
        return remote(ts.at[q], tin.at[q], tsend.at[q], trecv.at[q], {"sweep": mate})

    def pcopy():
        return remote(phi.at[core], phi.at[core], psend, precv, {"sweep": mate})

    def kcopy(d):
        return remote(phik.at[y], phik.at[y], ksend.at[d - 1], krecv.at[y], {"sweep": ring_peer(d)})

    def kland(d):
        k = lax.rem(y + RING - d, RING)
        return remote(phik.at[k], phik.at[k], ksend.at[d - 1], krecv.at[k], {"sweep": ring_peer(d)})

    loads[0].wait()
    loads[1].wait()
    for e in range(2):
        dbst[e, FACE:, :] = jnp.zeros((F - FACE, U), f32)
        for v in range(VARS):
            dbst[e, 25 * v:25 * v + 25, :] = bst[e, 125 * v + 100:125 * v + 125, :]
        hi, lo = halves(snust[e])
        sh[e] = hi
        sl[e] = lo
    dsnu = []
    dbs = []
    for e in range(2):
        hi, lo = halves(dbst[e])
        dbs.append((hi, lo))
        dsnu.append(dot(hi, sh[e]) + dot(hi, sl[e]) + dot(lo, sh[e]))
    m0 = dsnu[0][:, 2 * F:]
    m1 = dsnu[1][:, 2 * F:]
    m3[0] = left3(m0)
    m3[1] = left3(m1)
    dsn3[...] = left3(dsnu[0][:, :2 * F])
    gsn3[:, :6 * F] = left3(-dot(m3[1], right3(dsnu[0][:, :2 * F])))
    gsn3[:, 6 * F:] = left3(dsnu[1][:, :2 * F])
    phi[core] = dot(m3[1], right3(m0))
    pcopy().start()
    loads[2].wait()
    for e in range(2):
        hi, lo = halves(fst[e])
        fh[e] = hi
        fl[e] = lo
    df = []
    for e in range(2):
        hi, lo = dbs[e]
        df.append(dot(hi, fh[e]) + dot(hi, fl[e]) + dot(lo, fh[e]))
    gall = df[1] - dot(m3[1], right3(df[0]))
    for c in range(NP):
        g0f[c] = df[0][:, W * c:W * c + W]
        gf[c] = gall[:, W * c:W * c + W]
    pcopy().wait_recv()
    phi3[0] = left3(phi[0])
    phi3[1] = left3(phi[1])
    phik[y] = dot(phi3[1], right3(phi[0]))
    for d in (1, 2, 3):
        kcopy(d).start()

    def blocks():
        def one(n, _):
            e = n // 4
            rows = pl.ds(pl.multiple_of(lax.rem(n, 4) * 160, 160), 160)
            hi, lo = halves(bst[e, rows, :])
            r = dot(hi, sh[e]) + dot(hi, sl[e]) + dot(lo, sh[e])
            dfull[e, rows, :] = r
            bsn3[e, rows, :] = left3(r[:, :2 * F])
            bu3[e, rows, :] = left3(r[:, 2 * F:])
            r = dot(hi, fh[e]) + dot(hi, fl[e]) + dot(lo, fh[e])
            for c in range(NP):
                bfp[c, e, rows, :] = r[:, W * c:W * c + W]
            return 0

        lax.fori_loop(0, 8, one, 0)

    def face_rows():
        hst[FACE:F, :] = jnp.zeros((F - FACE, 3 * F), f32)
        hst[F + FACE:, :] = jnp.zeros((F - FACE, 3 * F), f32)

        def one(e, _):
            for g in range(25):
                hst[5 * g:5 * g + 5, :] = dfull[e, 25 * g + 20:25 * g + 25, :]
                hst[F + 5 * g:F + 5 * g + 5, :] = dfull[e, 25 * g:25 * g + 5, :]
            hsn3[e] = left3(hst[:, :2 * F])
            hu3[e] = left3(hst[:, 2 * F:])
            return 0

        lax.fori_loop(0, 2, one, 0)

        def two(n, _):
            c = n // 2
            e = lax.rem(n, 2)
            hlf[c, e, FACE:F, :] = jnp.zeros((F - FACE, W), f32)
            hlf[c, e, F + FACE:, :] = jnp.zeros((F - FACE, W), f32)
            for g in range(25):
                hlf[c, e, 5 * g:5 * g + 5, :] = bfp[c, e, 25 * g + 20:25 * g + 25, :]
                hlf[c, e, F + 5 * g:F + 5 * g + 5, :] = bfp[c, e, 25 * g:25 * g + 5, :]
            return 0

        lax.fori_loop(0, 2 * NP, two, 0)

    def coefficients():
        for d in (1, 2, 3):
            kland(d).wait_recv()
        eye = (lax.broadcasted_iota(jnp.int32, (F, F), 0) == lax.broadcasted_iota(jnp.int32, (F, F), 1)).astype(f32)
        coef[0] = eye
        coef[1] = eye

        def one(n, _):
            k = RING - 1 - n
            r = coef[0]
            s = coef[1]
            zero = jnp.zeros((F, F), f32)
            before = k < y
            a = jnp.where(before, r, zero)
            both = dot(left3(jnp.concatenate([r, s], axis=0)), right3(phik[k]))
            coef[0] = jnp.where(before, both[:F], r)
            coef[1] = both[F:]
            ua = dot(phi3[0], right3(a))
            col = pl.ds(pl.multiple_of(k * 3 * F, 3 * F), 3 * F)
            ca3[:, col] = left3(jnp.concatenate([a, ua, s], axis=0))
            return 0

        lax.fori_loop(0, RING, one, 0)
        e_map = coef[0]
        e3[:F, :] = left3(e_map)
        e3[F:, :] = left3(dot(phi3[0], right3(e_map)))

    def trace_in(q, c, lead):
        for way in range(2):
            zcopy2(q, way).wait_recv()
        for e in range(2):
            xq[q, e] = right3(jnp.concatenate([sn[q, 0, e], sn[q, 1, e]], axis=0))
        x0 = xq[q, 0]
        gown[q] = gf[c] - dot(gsn3[...], jnp.concatenate([x0, xq[q, 1]], axis=0))

        @pl.when(jnp.logical_not(lead))
        def _():
            gcopy(q).start()

        g0v[q] = g0f[c] - dot(dsn3[...], x0)

    def pair_up(q, c, lead):
        @pl.when(lead)
        def _():
            gcopy(q).wait_recv()
            own = gown[q]
            other = gpar[q]
            first = jnp.where(core == 0, own, other)
            second = jnp.where(core == 0, other, own)
            g0c[q] = first
            ag[q, y] = second + dot(phi3[1], right3(first))
            for d in (1, 2, 3):
                acopy(q, d).start()

    def settle(q, here, after):
        tin[q] = jnp.where(core == 0, here, after)
        ts[q] = jnp.where(core == 0, after, here)
        tcopy(q).start()

    def ring_sum(q, c, lead):
        @pl.when(lead)
        def _():
            for d in (1, 2, 3):
                aland(q, d).wait_recv()
            stack = jnp.concatenate([right3(ag[q, k]) for k in range(RING)], axis=0)
            r = dot(ca3[...], stack)

            @pl.when(x == 0)
            def _():
                xs[q] = r[2 * F:]
                xcopy(q).start()
                settle(q, r[:F], r[F:2 * F] + g0c[q])

            @pl.when(x == 1)
            def _():
                tp[q, 0] = r[:F]
                tp[q, 1] = r[F:2 * F] + g0c[q]

    def cross(q, c, lead):
        @pl.when(jnp.logical_and(lead, x == 1))
        def _():
            xcopy(q).wait_recv()
            r = dot(e3[...], right3(xb[q]))
            settle(q, tp[q, 0] + r[:F], tp[q, 1] + r[F:])

    def base(q, c, lead):
        @pl.when(q < NP)
        def _():
            for e in range(2):
                hb[c, e] = hlf[c, e] - dot(hsn3[e], xq[q, e])

        @pl.when(q >= NP)
        def _():
            for e in range(2):
                ob[c, e] = bfp[c, e, :UNK, :] - dot(bsn3[e], xq[q, e])[:UNK]

    def out_copy(c):
        return pltpu.make_async_copy(
            ob.at[c], out.at[:, :, pl.ds(pl.multiple_of(c * W, W), W)], out_sem.at[c]
        )

    def finish(q, c, lead):
        @pl.when(jnp.logical_not(lead))
        def _():
            tcopy(q).wait_recv()

        t0 = right3(tin[q])
        t1 = right3(g0v[q] - dot(m3[0], t0))

        @pl.when(q < NP)
        def _():
            for e, t in ((0, t0), (1, t1)):
                h = hb[c, e] - dot(hu3[e], t)
                zs[c, 0, e] = h[:F]
                zs[c, 1, e] = h[F:]
            for way in range(2):
                zcopy2(q + NP, way).start()

        @pl.when(q >= NP)
        def _():
            for e, t in ((0, t0), (1, t1)):
                ob[c, e] = ob[c, e] - dot(bu3[e], t)[:UNK]
            out_copy(c).start()

    gap = 6

    def slot(k, _):
        def at(behind, stage):
            n = k - behind
            active = jnp.logical_or(
                jnp.logical_and(n >= 0, n < NP), jnp.logical_and(n >= gap, n < gap + NP)
            )

            @pl.when(active)
            def _():
                late = (n >= gap).astype(jnp.int32)
                c = n - gap * late
                q = c + NP * late
                stage(q, c, core == lax.rem(c, 2))

        at(4, finish)
        at(3, cross)

        @pl.when(k == 2)
        def _():
            coefficients()

        at(2, ring_sum)
        at(2, base)
        at(1, pair_up)
        at(0, trace_in)

        @pl.when(k == 0)
        def _():
            blocks()

        @pl.when(k == 1)
        def _():
            face_rows()

        return 0

    lax.fori_loop(0, gap + NP + 4, slot, 0)

    pcopy().wait_send()
    for d in (1, 2, 3):
        kcopy(d).wait_send()

    def drain(q, _):
        for way in range(2):
            zcopy2(q, way).wait_send()
        lead = core == lax.rem(q, 2)

        @pl.when(lead)
        def _():
            for d in (1, 2, 3):
                acopy(q, d).wait_send()
            tcopy(q).wait_send()

            @pl.when(x == 0)
            def _():
                xcopy(q).wait_send()

        @pl.when(jnp.logical_not(lead))
        def _():
            gcopy(q).wait_send()

        return 0

    lax.fori_loop(0, NQ, drain, 0)
    for c in range(NP):
        out_copy(c).wait()


def solve(faces, b, snu, f):
    V = pltpu.VMEM
    D = pltpu.SemaphoreType.DMA
    scratch = [
        V((2, U, U), f32), V((2, U, 3 * F), f32), V((2, U, 512), f32),
        V((2, U, 3 * F), bf16), V((2, U, 3 * F), bf16),
        V((2, U, 512), bf16), V((2, U, 512), bf16), V((2, F, U), f32), V((2, U, 3 * F), f32),
        V((NP, 2, U, W), f32), V((2, U, 6 * F), bf16), V((2, U, 3 * F), bf16),
        V((2 * F, 3 * F), f32), V((2, 2 * F, 6 * F), bf16), V((2, 2 * F, 3 * F), bf16),
        V((NP, 2, 2 * F, W), f32),
        V((F, 12 * F), bf16), V((F, 6 * F), bf16), V((2, F, 3 * F), bf16), V((NP, F, W), f32),
        V((NP, F, W), f32), V((2, F, F), f32), V((RING, F, F), f32), V((2, F, F), f32),
        V((3 * F, 12 * F), bf16), V((2 * F, 3 * F), bf16), V((2, F, 3 * F), bf16),
        V((NQ, 2, 2, F, W), f32), V((NQ, 2, 6 * F, W), bf16), V((NQ, F, W), f32), V((NQ, F, W), f32),
        V((NQ, F, W), f32), V((NQ, F, W), f32), V((NQ, RING, F, W), f32), V((NQ, F, W), f32),
        V((NQ, F, W), f32), V((NQ, 2, F, W), f32), V((NQ, F, W), f32), V((NQ, F, W), f32),
        V((NP, 2, 2, F, W), f32), V((NP, 2, 2 * F, W), f32), V((NP, 2, UNK, W), f32),
        D((3,)), D((NP,)), D((NQ, 2)), D((NQ, 2)), D((NQ,)), D((NQ,)), D((NQ, 3)), D((NQ, RING)),
        D((NQ,)), D((NQ,)), D((NQ,)), D((NQ,)), D, D, D((3,)), D((RING,)),
    ]
    any_spec = pl.BlockSpec(memory_space=pl.ANY)
    return pl.pallas_call(
        kernel,
        out_shape=jax.ShapeDtypeStruct((2, UNK, 512), f32),
        in_specs=[any_spec] * 4,
        out_specs=any_spec,
        scratch_shapes=scratch,
        compiler_params=pltpu.CompilerParams(
            collective_id=0, has_side_effects=True, vmem_limit_bytes=60 * 1024 * 1024
        ),
    )(faces, b, snu, f)


def per_device(right_side, start_field, block_inverse, upwind_block, south_block, north_block):
    rows = (0, U - UNK)
    cols = (0, F - FACE)
    none = (0, 0)
    b = jnp.pad(block_inverse[:, 0], (none, rows, rows))
    parts = [jnp.pad(m[:, 0], (none, rows, cols)) for m in (south_block, north_block, upwind_block)]
    snu = jnp.concatenate(parts, axis=2)
    f = jnp.pad(right_side[:, 0], (none, rows, none))
    grid = start_field[:, 0].reshape(2, VARS * NODE, NODE, NODE, NP, W)
    faces = jnp.stack([grid[:, :, NODE - 1], grid[:, :, 0]])
    faces = jnp.transpose(faces.reshape(2, 2, FACE, NP, W), (0, 3, 1, 2, 4))
    faces = jnp.pad(faces, (none, none, none, cols, none))
    return solve(faces, b, snu, f)[:, None]


def solution(mesh):
    spec = P("sweep", "span", None, None)
    return jax.shard_map(
        per_device, mesh=mesh, in_specs=(spec,) * 6, out_specs=spec, check_vma=False
    )
```

```python
import jax
import jax.numpy as jnp
from jax import lax
from jax.experimental import pallas as pl
from jax.experimental.pallas import tpu as pltpu
from jax.sharding import PartitionSpec as P

VARS = 5
NODE = 5
UNK = 625
FACE = 125
F = 128
U = 640
W = 128
NP = 4
NQ = 2 * NP
RING = 4
MESH = pl.DeviceIdType.MESH
f32 = jnp.float32
bf16 = jnp.bfloat16


def dot(a, b):
    return jnp.dot(a, b, preferred_element_type=f32)


def halves(x):
    hi = x.astype(bf16)
    lo = (x - hi.astype(f32)).astype(bf16)
    return hi, lo


def left3(x):
    hi, lo = halves(x)
    return jnp.concatenate([hi, lo, hi], axis=1)


def right3(x):
    hi, lo = halves(x)
    return jnp.concatenate([hi, hi, lo], axis=0)


def product(a, b):
    return dot(left3(a), right3(b))


def kernel(
    start, b_in, s_in, n_in, u_in, f_in,
    out,
    bst, sust, fst, sh, sl, fh, fl, dbst, hbst, bch, bcl, bfp, bsn3, bu3, hsn3, hu3, hlf, snr,
    gsn3, dsn3, m3, gf, g0f, phi, phik, coef, ca3, e3, phi3,
    sn, xq, gown, gpar, g0c, g0v, ag, xs, xb, tp, tin, ts, zs, hb, ob,
    load_sem, out_sem, zsend, zrecv, gsend, grecv, asend, arecv, xsend, xrecv, tsend, trecv,
    psend, precv, ksend, krecv,
):
    p = lax.axis_index("sweep")
    j = lax.axis_index("span")
    span = 16
    core = lax.rem(p, 2)
    chip = p // 2
    y = lax.rem(chip, RING)
    x = chip // RING
    mate = p + 1 - 2 * core
    up = lax.rem(j + 1, span)
    down = lax.rem(j + span - 1, span)

    def ring_peer(d):
        return (x * RING + lax.rem(y + d, RING)) * 2 + core

    over = lax.rem(p + 8, 16)

    def load(src, dst, n):
        return pltpu.make_async_copy(src, dst, load_sem.at[n])

    barrier = pltpu.get_barrier_semaphore()
    for dev in ({"span": up}, {"span": down}, {"sweep": mate}, {"sweep": over},
                {"sweep": ring_peer(1)}, {"sweep": ring_peer(2)}, {"sweep": ring_peer(3)}):
        pl.semaphore_signal(barrier, inc=1, device_id=dev, device_id_type=MESH)
    pl.semaphore_wait(barrier, 7)

    def remote(src, dst, ss, rs, dev):
        return pltpu.make_async_remote_copy(
            src_ref=src, dst_ref=dst, send_sem=ss, recv_sem=rs, device_id=dev, device_id_type=MESH
        )

    def zdev(way):
        return {"span": up if way == 0 else down}

    def zcopy1(c, way):
        level = NODE - 1 if way == 0 else 0
        src = start.at[:, :, level, :, 0, pl.ds(pl.multiple_of(c * W, W), W)]
        return remote(src, snr.at[c, way], zsend.at[c, way], zrecv.at[c, way], zdev(way))

    def zcopy2(q, way):
        c = lax.rem(q, NP)
        return remote(zs.at[c, way], sn.at[q, way], zsend.at[q, way], zrecv.at[q, way], zdev(way))

    for c in range(NP):
        for way in range(2):
            zcopy1(c, way).start()
    def gcopy(q):
        return remote(gown.at[q], gpar.at[q], gsend.at[q], grecv.at[q], {"sweep": mate})

    def acopy(q, d):
        return remote(ag.at[q, y], ag.at[q, y], asend.at[q, d - 1], arecv.at[q, y], {"sweep": ring_peer(d)})

    def aland(q, d):
        k = lax.rem(y + RING - d, RING)
        return remote(ag.at[q, k], ag.at[q, k], asend.at[q, d - 1], arecv.at[q, k], {"sweep": ring_peer(d)})

    def xcopy(q):
        return remote(xs.at[q], xb.at[q], xsend.at[q], xrecv.at[q], {"sweep": over})

    def tcopy(q):
        return remote(ts.at[q], tin.at[q], tsend.at[q], trecv.at[q], {"sweep": mate})

    def pcopy():
        return remote(phi.at[core], phi.at[core], psend, precv, {"sweep": mate})

    def kcopy(d):
        return remote(phik.at[y], phik.at[y], ksend.at[d - 1], krecv.at[y], {"sweep": ring_peer(d)})

    def kland(d):
        k = lax.rem(y + RING - d, RING)
        return remote(phik.at[k], phik.at[k], ksend.at[d - 1], krecv.at[k], {"sweep": ring_peer(d)})

    b_load = load(b_in.at[:, :, 0, :], bst, 0)
    b_load.start()
    su_loads = [load(m.at[:, :, 0, :], sust.at[n], 1 + n) for n, m in enumerate((s_in, n_in, u_in))]
    for c in su_loads:
        c.start()
    f_load = load(f_in.at[:, :, 0, :], fst, 4)
    f_load.start()

    edge = pl.ds(U - F, F)
    hbst[:, edge] = jnp.zeros((2 * F, F), f32)
    hbst[FACE:F, :] = jnp.zeros((F - FACE, U), f32)
    hbst[F + FACE:, :] = jnp.zeros((F - FACE, U), f32)
    bch[:, edge] = jnp.zeros((160, F), bf16)
    bcl[:, edge] = jnp.zeros((160, F), bf16)
    for e in range(2):
        dbst[e, :, edge] = jnp.zeros((F, F), f32)
        dbst[e, FACE:, :] = jnp.zeros((F - FACE, U), f32)
        for ref in (sh, sl):
            ref[e] = jnp.zeros((U, 3 * F), bf16)
        for ref in (fh, fl):
            ref[e, U - 16:, :] = jnp.zeros((16, 512), bf16)

    b_load.wait()
    for e in range(2):
        for v in range(VARS):
            dbst[e, 25 * v:25 * v + 25, :UNK] = bst[e, 125 * v + 100:125 * v + 125, :]
    for n in range(3):
        su_loads[n].wait()
        for e in range(2):
            hi, lo = halves(sust[n, e])
            sh[e, :UNK, F * n:F * n + FACE] = hi
            sl[e, :UNK, F * n:F * n + FACE] = lo
    dsnu = []
    dbs = []
    for e in range(2):
        hi, lo = halves(dbst[e])
        dbs.append((hi, lo))
        dsnu.append(dot(hi, sh[e]) + dot(hi, sl[e]) + dot(lo, sh[e]))
    m0 = dsnu[0][:, 2 * F:]
    m1 = dsnu[1][:, 2 * F:]
    m3[0] = left3(m0)
    m3[1] = left3(m1)
    dsn3[...] = left3(dsnu[0][:, :2 * F])
    gsn3[:, :6 * F] = left3(-dot(m3[1], right3(dsnu[0][:, :2 * F])))
    gsn3[:, 6 * F:] = left3(dsnu[1][:, :2 * F])
    phi[core] = dot(m3[1], right3(m0))
    pcopy().start()
    f_load.wait()
    for e in range(2):
        hi, lo = halves(fst[e])
        fh[e, :UNK, :] = hi
        fl[e, :UNK, :] = lo
    df = []
    for e in range(2):
        hi, lo = dbs[e]
        df.append(dot(hi, fh[e]) + dot(hi, fl[e]) + dot(lo, fh[e]))
    gall = df[1] - dot(m3[1], right3(df[0]))
    for c in range(NP):
        g0f[c] = df[0][:, W * c:W * c + W]
        gf[c] = gall[:, W * c:W * c + W]
    pcopy().wait_recv()
    phi3[0] = left3(phi[0])
    phi3[1] = left3(phi[1])
    phik[y] = dot(phi3[1], right3(phi[0]))
    for d in (1, 2, 3):
        kcopy(d).start()

    def blocks(start_at):
        def one(i, _):
            n = start_at + i
            e = n // 4
            m = lax.rem(n, 4)
            rows = pl.ds(pl.multiple_of(m * 160, 160), 160)

            @pl.when(m < 3)
            def _():
                hi, lo = halves(bst[e, rows, :])
                bch[:, :UNK] = hi
                bcl[:, :UNK] = lo

            @pl.when(m == 3)
            def _():
                hi, lo = halves(bst[e, 480:UNK, :])
                bch[:UNK - 480, :UNK] = hi
                bcl[:UNK - 480, :UNK] = lo

            hi = bch[...]
            lo = bcl[...]
            r = dot(hi, sh[e]) + dot(hi, sl[e]) + dot(lo, sh[e])
            bsn3[e, rows, :] = left3(r[:, :2 * F])
            bu3[e, rows, :] = left3(r[:, 2 * F:])
            r = dot(hi, fh[e]) + dot(hi, fl[e]) + dot(lo, fh[e])
            for c in range(NP):
                bfp[c, e, rows, :] = r[:, W * c:W * c + W]
            return 0

        lax.fori_loop(0, 2, one, 0)

    def face_rows(e):
        for g in range(25):
            hbst[5 * g:5 * g + 5, :UNK] = bst[e, 25 * g + 20:25 * g + 25, :]
            hbst[F + 5 * g:F + 5 * g + 5, :UNK] = bst[e, 25 * g:25 * g + 5, :]
        hi, lo = halves(hbst[...])
        r = dot(hi, sh[e]) + dot(hi, sl[e]) + dot(lo, sh[e])
        hsn3[e] = left3(r[:, :2 * F])
        hu3[e] = left3(r[:, 2 * F:])
        r = dot(hi, fh[e]) + dot(hi, fl[e]) + dot(lo, fh[e])
        for c in range(NP):
            hlf[c, e] = r[:, W * c:W * c + W]

    def coefficients():
        for d in (1, 2, 3):
            kland(d).wait_recv()
        eye = (lax.broadcasted_iota(jnp.int32, (F, F), 0) == lax.broadcasted_iota(jnp.int32, (F, F), 1)).astype(f32)
        coef[0] = eye
        coef[1] = eye

        def one(n, _):
            k = RING - 1 - n
            r = coef[0]
            s = coef[1]
            zero = jnp.zeros((F, F), f32)
            before = k < y
            a = jnp.where(before, r, zero)
            both = dot(left3(jnp.concatenate([r, s], axis=0)), right3(phik[k]))
            coef[0] = jnp.where(before, both[:F], r)
            coef[1] = both[F:]
            ua = dot(phi3[0], right3(a))
            col = pl.ds(pl.multiple_of(k * 3 * F, 3 * F), 3 * F)
            ca3[:, col] = left3(jnp.concatenate([a, ua, s], axis=0))
            return 0

        lax.fori_loop(0, RING, one, 0)
        e_map = coef[0]
        e3[:F, :] = left3(e_map)
        e3[F:, :] = left3(dot(phi3[0], right3(e_map)))

    def trace_in(q, c, lead):
        @pl.when(q < NP)
        def _():
            for way in range(2):
                zcopy1(c, way).wait_recv()
                for e in range(2):
                    sn[q, way, e, FACE:, :] = jnp.zeros((F - FACE, W), f32)
                    for g in range(25):
                        sn[q, way, e, 5 * g:5 * g + 5, :] = snr[c, way, e, g]

        @pl.when(q >= NP)
        def _():
            for way in range(2):
                zcopy2(q, way).wait_recv()

        for e in range(2):
            xq[q, e] = right3(jnp.concatenate([sn[q, 0, e], sn[q, 1, e]], axis=0))
        x0 = xq[q, 0]
        gown[q] = gf[c] - dot(gsn3[...], jnp.concatenate([x0, xq[q, 1]], axis=0))

        @pl.when(jnp.logical_not(lead))
        def _():
            gcopy(q).start()

        g0v[q] = g0f[c] - dot(dsn3[...], x0)

    def pair_up(q, c, lead):
        @pl.when(lead)
        def _():
            gcopy(q).wait_recv()
            own = gown[q]
            other = gpar[q]
            first = jnp.where(core == 0, own, other)
            second = jnp.where(core == 0, other, own)
            g0c[q] = first
            ag[q, y] = second + dot(phi3[1], right3(first))
            for d in (1, 2, 3):
                acopy(q, d).start()

    def settle(q, here, after):
        tin[q] = jnp.where(core == 0, here, after)
        ts[q] = jnp.where(core == 0, after, here)
        tcopy(q).start()

    def ring_sum(q, c, lead):
        @pl.when(lead)
        def _():
            for d in (1, 2, 3):
                aland(q, d).wait_recv()
            stack = jnp.concatenate([right3(ag[q, k]) for k in range(RING)], axis=0)
            r = dot(ca3[...], stack)

            @pl.when(x == 0)
            def _():
                xs[q] = r[2 * F:]
                xcopy(q).start()
                settle(q, r[:F], r[F:2 * F] + g0c[q])

            @pl.when(x == 1)
            def _():
                tp[q, 0] = r[:F]
                tp[q, 1] = r[F:2 * F] + g0c[q]

    def cross(q, c, lead):
        @pl.when(jnp.logical_and(lead, x == 1))
        def _():
            xcopy(q).wait_recv()
            r = dot(e3[...], right3(xb[q]))
            settle(q, tp[q, 0] + r[:F], tp[q, 1] + r[F:])

    def base1(q, c, lead):
        @pl.when(q < NP)
        def _():
            for e in range(2):
                hb[c, e] = hlf[c, e] - dot(hsn3[e], xq[q, e])

    def base2(q, c, lead):
        @pl.when(q >= NP)
        def _():
            for e in range(2):
                ob[c, e] = bfp[c, e, :UNK, :] - dot(bsn3[e], xq[q, e])[:UNK]

    def out_copy(c):
        return pltpu.make_async_copy(
            ob.at[c], out.at[:, :, 0, pl.ds(pl.multiple_of(c * W, W), W)], out_sem.at[c]
        )

    def finish(q, c, lead):
        @pl.when(jnp.logical_not(lead))
        def _():
            tcopy(q).wait_recv()

        t0 = right3(tin[q])
        t1 = right3(g0v[q] - dot(m3[0], t0))

        @pl.when(q < NP)
        def _():
            for e, t in ((0, t0), (1, t1)):
                h = hb[c, e] - dot(hu3[e], t)
                zs[c, 0, e] = h[:F]
                zs[c, 1, e] = h[F:]
            for way in range(2):
                zcopy2(q + NP, way).start()

        @pl.when(q >= NP)
        def _():
            for e, t in ((0, t0), (1, t1)):
                ob[c, e] = ob[c, e] - dot(bu3[e], t)[:UNK]
            out_copy(c).start()

    gap = 6

    def slot(k, _):
        def at(behind, stage):
            n = k - behind
            active = jnp.logical_or(
                jnp.logical_and(n >= 0, n < NP), jnp.logical_and(n >= gap, n < gap + NP)
            )

            @pl.when(active)
            def _():
                late = (n >= gap).astype(jnp.int32)
                c = n - gap * late
                q = c + NP * late
                stage(q, c, core == lax.rem(c, 2))

        at(4, finish)
        at(3, cross)
        at(3, base1)
        at(2, ring_sum)
        at(2, base2)
        at(1, pair_up)
        at(0, trace_in)

        @pl.when(k == 1)
        def _():
            coefficients()

        @pl.when(k < 2)
        def _():
            face_rows(k)

        @pl.when(jnp.logical_and(k >= 4, k < 8))
        def _():
            blocks(2 * (k - 4))

        return 0

    lax.fori_loop(0, gap + NP + 4, slot, 0)

    pcopy().wait_send()
    for c in range(NP):
        for way in range(2):
            zcopy1(c, way).wait_send()
            zcopy2(c + NP, way).wait_send()
    for d in (1, 2, 3):
        kcopy(d).wait_send()

    def drain(q, _):
        lead = core == lax.rem(q, 2)

        @pl.when(lead)
        def _():
            for d in (1, 2, 3):
                acopy(q, d).wait_send()
            tcopy(q).wait_send()

            @pl.when(x == 0)
            def _():
                xcopy(q).wait_send()

        @pl.when(jnp.logical_not(lead))
        def _():
            gcopy(q).wait_send()

        return 0

    lax.fori_loop(0, NQ, drain, 0)
    for c in range(NP):
        out_copy(c).wait()


def solve(*args):
    V = pltpu.VMEM
    D = pltpu.SemaphoreType.DMA
    scratch = [
        V((2, UNK, UNK), f32), V((3, 2, UNK, FACE), f32), V((2, UNK, 512), f32),
        V((2, U, 3 * F), bf16), V((2, U, 3 * F), bf16), V((2, U, 512), bf16), V((2, U, 512), bf16),
        V((2, F, U), f32), V((2 * F, U), f32), V((160, U), bf16), V((160, U), bf16),
        V((NP, 2, U, W), f32), V((2, U, 6 * F), bf16), V((2, U, 3 * F), bf16),
        V((2, 2 * F, 6 * F), bf16), V((2, 2 * F, 3 * F), bf16), V((NP, 2, 2 * F, W), f32),
        V((NP, 2, 2, 25, NODE, W), f32),
        V((F, 12 * F), bf16), V((F, 6 * F), bf16), V((2, F, 3 * F), bf16), V((NP, F, W), f32),
        V((NP, F, W), f32), V((2, F, F), f32), V((RING, F, F), f32), V((2, F, F), f32),
        V((3 * F, 12 * F), bf16), V((2 * F, 3 * F), bf16), V((2, F, 3 * F), bf16),
        V((NQ, 2, 2, F, W), f32), V((NQ, 2, 6 * F, W), bf16), V((NQ, F, W), f32), V((NQ, F, W), f32),
        V((NQ, F, W), f32), V((NQ, F, W), f32), V((NQ, RING, F, W), f32), V((NQ, F, W), f32),
        V((NQ, F, W), f32), V((NQ, 2, F, W), f32), V((NQ, F, W), f32), V((NQ, F, W), f32),
        V((NP, 2, 2, F, W), f32), V((NP, 2, 2 * F, W), f32), V((NP, 2, UNK, W), f32),
        D((5,)), D((NP,)), D((NQ, 2)), D((NQ, 2)), D((NQ,)), D((NQ,)), D((NQ, 3)), D((NQ, RING)),
        D((NQ,)), D((NQ,)), D((NQ,)), D((NQ,)), D, D, D((3,)), D((RING,)),
    ]
    any_spec = pl.BlockSpec(memory_space=pl.ANY)
    return pl.pallas_call(
        kernel,
        out_shape=jax.ShapeDtypeStruct((2, UNK, 1, 512), f32),
        in_specs=[any_spec] * 6,
        out_specs=any_spec,
        scratch_shapes=scratch,
        compiler_params=pltpu.CompilerParams(
            collective_id=0, has_side_effects=True, vmem_limit_bytes=60 * 1024 * 1024
        ),
    )(*args)


def per_device(right_side, start_field, block_inverse, upwind_block, south_block, north_block):
    def rows_first(a):
        return jnp.transpose(a, (0, 2, 1, 3))

    grid = rows_first(start_field).reshape(2, VARS * NODE, NODE, NODE, 1, 512)
    rest = [rows_first(a) for a in (block_inverse, south_block, north_block, upwind_block, right_side)]
    return rows_first(solve(grid, *rest))


def solution(mesh):
    spec = P("sweep", "span", None, None)
    return jax.shard_map(
        per_device, mesh=mesh, in_specs=(spec,) * 6, out_specs=spec, check_vma=False
    )
```

```python
import jax
import jax.numpy as jnp
from jax import lax
from jax.experimental import pallas as pl
from jax.experimental.pallas import tpu as pltpu
from jax.sharding import PartitionSpec as P

VARS = 5
NODE = 5
UNK = 625
FACE = 125
F = 128
U = 640
W = 128
NP = 4
NQ = 2 * NP
RING = 4
MESH = pl.DeviceIdType.MESH
f32 = jnp.float32
bf16 = jnp.bfloat16


def dot(a, b):
    return jnp.dot(a, b, preferred_element_type=f32)


def halves(x):
    hi = x.astype(bf16)
    lo = (x - hi.astype(f32)).astype(bf16)
    return hi, lo


def left3(x):
    hi, lo = halves(x)
    return jnp.concatenate([hi, lo, hi], axis=1)


def right3(x):
    hi, lo = halves(x)
    return jnp.concatenate([hi, hi, lo], axis=0)


def product(a, b):
    return dot(left3(a), right3(b))


def kernel(
    start, b_in, s_in, n_in, u_in, f_in,
    out,
    bst, sust, fst, sh, sl, fh, fl, dbst, hbst, bch, bcl, bfp, bsn3, bu3, hsn3, hu3, hlf, snr,
    gsn3, dsn3, m3, gf, g0f, phi, phik, coef, ca3, e3, phi3,
    sn, xq, gown, gpar, g0c, g0v, ag, xs, xb, tp, tin, ts, zs, hb, ob,
    load_sem, out_sem, zsend, zrecv, gsend, grecv, asend, arecv, xsend, xrecv, tsend, trecv,
    psend, precv, ksend, krecv,
):
    p = lax.axis_index("sweep")
    j = lax.axis_index("span")
    span = 16
    core = lax.rem(p, 2)
    chip = p // 2
    y = lax.rem(chip, RING)
    x = chip // RING
    mate = p + 1 - 2 * core
    up = lax.rem(j + 1, span)
    down = lax.rem(j + span - 1, span)

    def ring_peer(d):
        return (x * RING + lax.rem(y + d, RING)) * 2 + core

    over = lax.rem(p + 8, 16)

    def load(src, dst, n):
        return pltpu.make_async_copy(src, dst, load_sem.at[n])

    barrier = pltpu.get_barrier_semaphore()
    for dev in ({"span": up}, {"span": down}, {"sweep": mate}, {"sweep": over},
                {"sweep": ring_peer(1)}, {"sweep": ring_peer(2)}, {"sweep": ring_peer(3)}):
        pl.semaphore_signal(barrier, inc=1, device_id=dev, device_id_type=MESH)
    pl.semaphore_wait(barrier, 7)

    def remote(src, dst, ss, rs, dev):
        return pltpu.make_async_remote_copy(
            src_ref=src, dst_ref=dst, send_sem=ss, recv_sem=rs, device_id=dev, device_id_type=MESH
        )

    def zdev(way):
        return {"span": up if way == 0 else down}

    def zcopy1(c, way):
        level = NODE - 1 if way == 0 else 0
        src = start.at[:, :, level, :, 0, pl.ds(pl.multiple_of(c * W, W), W)]
        return remote(src, snr.at[c, way], zsend.at[c, way], zrecv.at[c, way], zdev(way))

    def zcopy2(q, way):
        c = lax.rem(q, NP)
        return remote(zs.at[c, way], sn.at[q, way], zsend.at[q, way], zrecv.at[q, way], zdev(way))

    for c in range(NP):
        for way in range(2):
            zcopy1(c, way).start()
    def gcopy(q):
        return remote(gown.at[q], gpar.at[q], gsend.at[q], grecv.at[q], {"sweep": mate})

    def acopy(q, d):
        return remote(ag.at[q, y], ag.at[q, y], asend.at[q, d - 1], arecv.at[q, y], {"sweep": ring_peer(d)})

    def aland(q, d):
        k = lax.rem(y + RING - d, RING)
        return remote(ag.at[q, k], ag.at[q, k], asend.at[q, d - 1], arecv.at[q, k], {"sweep": ring_peer(d)})

    def xcopy(q):
        return remote(xs.at[q], xb.at[q], xsend.at[q], xrecv.at[q], {"sweep": over})

    def tcopy(q):
        return remote(ts.at[q], tin.at[q], tsend.at[q], trecv.at[q], {"sweep": mate})

    def pcopy():
        return remote(phi.at[core], phi.at[core], psend, precv, {"sweep": mate})

    def kcopy(d):
        return remote(phik.at[y], phik.at[y], ksend.at[d - 1], krecv.at[y], {"sweep": ring_peer(d)})

    def kland(d):
        k = lax.rem(y + RING - d, RING)
        return remote(phik.at[k], phik.at[k], ksend.at[d - 1], krecv.at[k], {"sweep": ring_peer(d)})

    b_load = load(b_in.at[:, :, 0, :], bst, 0)
    b_load.start()
    su_loads = [load(m.at[:, :, 0, :], sust.at[n], 1 + n) for n, m in enumerate((s_in, n_in, u_in))]
    for c in su_loads:
        c.start()
    f_load = load(f_in.at[:, :, 0, :], fst, 4)
    f_load.start()

    edge = pl.ds(U - F, F)
    hbst[:, edge] = jnp.zeros((2 * F, F), f32)
    hbst[FACE:F, :] = jnp.zeros((F - FACE, U), f32)
    hbst[F + FACE:, :] = jnp.zeros((F - FACE, U), f32)
    bch[:, edge] = jnp.zeros((160, F), bf16)
    bcl[:, edge] = jnp.zeros((160, F), bf16)
    for e in range(2):
        dbst[e, :, edge] = jnp.zeros((F, F), f32)
        dbst[e, FACE:, :] = jnp.zeros((F - FACE, U), f32)
        for ref in (sh, sl):
            ref[e] = jnp.zeros((U, 3 * F), bf16)
        for ref in (fh, fl):
            ref[e, U - 16:, :] = jnp.zeros((16, 512), bf16)

    b_load.wait()
    for e in range(2):
        for v in range(VARS):
            dbst[e, 25 * v:25 * v + 25, :UNK] = bst[e, 125 * v + 100:125 * v + 125, :]
    for n in range(3):
        su_loads[n].wait()
        for e in range(2):
            hi, lo = halves(sust[n, e])
            sh[e, :UNK, F * n:F * n + FACE] = hi
            sl[e, :UNK, F * n:F * n + FACE] = lo
    dsnu = []
    dbs = []
    for e in range(2):
        hi, lo = halves(dbst[e])
        dbs.append((hi, lo))
        dsnu.append(dot(hi, sh[e]) + dot(hi, sl[e]) + dot(lo, sh[e]))
    m0 = dsnu[0][:, 2 * F:]
    m1 = dsnu[1][:, 2 * F:]
    m3[0] = left3(m0)
    m3[1] = left3(m1)
    dsn3[...] = left3(dsnu[0][:, :2 * F])
    gsn3[:, :6 * F] = left3(-dot(m3[1], right3(dsnu[0][:, :2 * F])))
    gsn3[:, 6 * F:] = left3(dsnu[1][:, :2 * F])
    phi[core] = dot(m3[1], right3(m0))
    pcopy().start()
    f_load.wait()
    for e in range(2):
        hi, lo = halves(fst[e])
        fh[e, :UNK, :] = hi
        fl[e, :UNK, :] = lo
    df = []
    for e in range(2):
        hi, lo = dbs[e]
        df.append(dot(hi, fh[e]) + dot(hi, fl[e]) + dot(lo, fh[e]))
    gall = df[1] - dot(m3[1], right3(df[0]))
    for c in range(NP):
        g0f[c] = df[0][:, W * c:W * c + W]
        gf[c] = gall[:, W * c:W * c + W]
    pcopy().wait_recv()
    phi3[0] = left3(phi[0])
    phi3[1] = left3(phi[1])
    phik[y] = dot(phi3[1], right3(phi[0]))
    for d in (1, 2, 3):
        kcopy(d).start()

    def blocks(start_at):
        def one(i, _):
            n = start_at + i
            e = n // 4
            m = lax.rem(n, 4)
            rows = pl.ds(pl.multiple_of(m * 160, 160), 160)

            @pl.when(m < 3)
            def _():
                hi, lo = halves(bst[e, rows, :])
                bch[:, :UNK] = hi
                bcl[:, :UNK] = lo

            @pl.when(m == 3)
            def _():
                hi, lo = halves(bst[e, 480:UNK, :])
                bch[:UNK - 480, :UNK] = hi
                bcl[:UNK - 480, :UNK] = lo

            hi = bch[...]
            lo = bcl[...]
            r = dot(hi, sh[e]) + dot(hi, sl[e]) + dot(lo, sh[e])
            bsn3[e, rows, :] = left3(r[:, :2 * F])
            bu3[e, rows, :] = left3(r[:, 2 * F:])
            r = dot(hi, fh[e]) + dot(hi, fl[e]) + dot(lo, fh[e])
            for c in range(NP):
                bfp[c, e, rows, :] = r[:, W * c:W * c + W]
            return 0

        lax.fori_loop(0, 1, one, 0)

    def face_rows(e):
        for g in range(25):
            hbst[5 * g:5 * g + 5, :UNK] = bst[e, 25 * g + 20:25 * g + 25, :]
            hbst[F + 5 * g:F + 5 * g + 5, :UNK] = bst[e, 25 * g:25 * g + 5, :]
        hi, lo = halves(hbst[...])
        r = dot(hi, sh[e]) + dot(hi, sl[e]) + dot(lo, sh[e])
        hsn3[e] = left3(r[:, :2 * F])
        hu3[e] = left3(r[:, 2 * F:])
        r = dot(hi, fh[e]) + dot(hi, fl[e]) + dot(lo, fh[e])
        for c in range(NP):
            hlf[c, e] = r[:, W * c:W * c + W]

    def coefficients():
        for d in (1, 2, 3):
            kland(d).wait_recv()
        eye = (lax.broadcasted_iota(jnp.int32, (F, F), 0) == lax.broadcasted_iota(jnp.int32, (F, F), 1)).astype(f32)
        coef[0] = eye
        coef[1] = eye

        def one(n, _):
            k = RING - 1 - n
            r = coef[0]
            s = coef[1]
            zero = jnp.zeros((F, F), f32)
            before = k < y
            a = jnp.where(before, r, zero)
            both = dot(left3(jnp.concatenate([r, s], axis=0)), right3(phik[k]))
            coef[0] = jnp.where(before, both[:F], r)
            coef[1] = both[F:]
            ua = dot(phi3[0], right3(a))
            col = pl.ds(pl.multiple_of(k * 3 * F, 3 * F), 3 * F)
            ca3[:, col] = left3(jnp.concatenate([a, ua, s], axis=0))
            return 0

        lax.fori_loop(0, RING, one, 0)
        e_map = coef[0]
        e3[:F, :] = left3(e_map)
        e3[F:, :] = left3(dot(phi3[0], right3(e_map)))

    def trace_in(q, c, lead):
        @pl.when(q < NP)
        def _():
            for way in range(2):
                zcopy1(c, way).wait_recv()
                for e in range(2):
                    sn[q, way, e, FACE:, :] = jnp.zeros((F - FACE, W), f32)
                    for g in range(25):
                        sn[q, way, e, 5 * g:5 * g + 5, :] = snr[c, way, e, g]

        @pl.when(q >= NP)
        def _():
            for way in range(2):
                zcopy2(q, way).wait_recv()

        for e in range(2):
            xq[q, e] = right3(jnp.concatenate([sn[q, 0, e], sn[q, 1, e]], axis=0))
        x0 = xq[q, 0]
        gown[q] = gf[c] - dot(gsn3[...], jnp.concatenate([x0, xq[q, 1]], axis=0))

        @pl.when(jnp.logical_not(lead))
        def _():
            gcopy(q).start()

        g0v[q] = g0f[c] - dot(dsn3[...], x0)

    def pair_up(q, c, lead):
        @pl.when(lead)
        def _():
            gcopy(q).wait_recv()
            own = gown[q]
            other = gpar[q]
            first = jnp.where(core == 0, own, other)
            second = jnp.where(core == 0, other, own)
            g0c[q] = first
            ag[q, y] = second + dot(phi3[1], right3(first))
            for d in (2, 1, 3):
                acopy(q, d).start()

    def settle(q, here, after):
        tin[q] = jnp.where(core == 0, here, after)
        ts[q] = jnp.where(core == 0, after, here)
        tcopy(q).start()

    def ring_sum(q, c, lead):
        @pl.when(lead)
        def _():
            for d in (1, 2, 3):
                aland(q, d).wait_recv()
            stack = jnp.concatenate([right3(ag[q, k]) for k in range(RING)], axis=0)
            r = dot(ca3[...], stack)

            @pl.when(x == 0)
            def _():
                xs[q] = r[2 * F:]
                xcopy(q).start()
                settle(q, r[:F], r[F:2 * F] + g0c[q])

            @pl.when(x == 1)
            def _():
                tp[q, 0] = r[:F]
                tp[q, 1] = r[F:2 * F] + g0c[q]

    def cross(q, c, lead):
        @pl.when(jnp.logical_and(lead, x == 1))
        def _():
            xcopy(q).wait_recv()
            r = dot(e3[...], right3(xb[q]))
            settle(q, tp[q, 0] + r[:F], tp[q, 1] + r[F:])

    def base1(q, c, lead):
        @pl.when(q < NP)
        def _():
            for e in range(2):
                hb[c, e] = hlf[c, e] - dot(hsn3[e], xq[q, e])

    def base2(q, c, lead):
        @pl.when(q >= NP)
        def _():
            for e in range(2):
                ob[c, e] = bfp[c, e, :UNK, :] - dot(bsn3[e], xq[q, e])[:UNK]

    def out_copy(c):
        return pltpu.make_async_copy(
            ob.at[c], out.at[c], out_sem.at[c]
        )

    def finish(q, c, lead):
        @pl.when(jnp.logical_not(lead))
        def _():
            tcopy(q).wait_recv()

        t0 = right3(tin[q])
        t1 = right3(g0v[q] - dot(m3[0], t0))

        @pl.when(q < NP)
        def _():
            for e, t in ((0, t0), (1, t1)):
                h = hb[c, e] - dot(hu3[e], t)
                zs[c, 0, e] = h[:F]
                zs[c, 1, e] = h[F:]
            for way in range(2):
                zcopy2(q + NP, way).start()

        @pl.when(q >= NP)
        def _():
            for e, t in ((0, t0), (1, t1)):
                ob[c, e] = ob[c, e] - dot(bu3[e], t)[:UNK]
            out_copy(c).start()

    gap = 7

    def slot(k, _):
        def at(behind, stage):
            n = k - behind
            active = jnp.logical_or(
                jnp.logical_and(n >= 0, n < NP), jnp.logical_and(n >= gap, n < gap + NP)
            )

            @pl.when(active)
            def _():
                late = (n >= gap).astype(jnp.int32)
                c = n - gap * late
                q = c + NP * late
                stage(q, c, core == lax.rem(c, 2))

        at(5, finish)
        at(4, cross)
        at(4, base1)
        at(3, ring_sum)
        at(3, base2)
        at(1, pair_up)
        at(0, trace_in)
        @pl.when(k == 1)
        def _():
            coefficients()

        @pl.when(k < 2)
        def _():
            face_rows(k)

        @pl.when(jnp.logical_and(k >= 2, k < 10))
        def _():
            blocks(k - 2)


        return 0

    lax.fori_loop(0, gap + NP + 5, slot, 0)

    pcopy().wait_send()
    for c in range(NP):
        for way in range(2):
            zcopy1(c, way).wait_send()
            zcopy2(c + NP, way).wait_send()
    for d in (1, 2, 3):
        kcopy(d).wait_send()

    def drain(q, _):
        lead = core == lax.rem(q, 2)

        @pl.when(lead)
        def _():
            for d in (1, 2, 3):
                acopy(q, d).wait_send()
            tcopy(q).wait_send()

            @pl.when(x == 0)
            def _():
                xcopy(q).wait_send()

        @pl.when(jnp.logical_not(lead))
        def _():
            gcopy(q).wait_send()

        return 0

    lax.fori_loop(0, NQ, drain, 0)
    for c in range(NP):
        out_copy(c).wait()


def solve(*args):
    V = pltpu.VMEM
    D = pltpu.SemaphoreType.DMA
    scratch = [
        V((2, UNK, UNK), f32), V((3, 2, UNK, FACE), f32), V((2, UNK, 512), f32),
        V((2, U, 3 * F), bf16), V((2, U, 3 * F), bf16), V((2, U, 512), bf16), V((2, U, 512), bf16),
        V((2, F, U), f32), V((2 * F, U), f32), V((160, U), bf16), V((160, U), bf16),
        V((NP, 2, U, W), f32), V((2, U, 6 * F), bf16), V((2, U, 3 * F), bf16),
        V((2, 2 * F, 6 * F), bf16), V((2, 2 * F, 3 * F), bf16), V((NP, 2, 2 * F, W), f32),
        V((NP, 2, 2, 25, NODE, W), f32),
        V((F, 12 * F), bf16), V((F, 6 * F), bf16), V((2, F, 3 * F), bf16), V((NP, F, W), f32),
        V((NP, F, W), f32), V((2, F, F), f32), V((RING, F, F), f32), V((2, F, F), f32),
        V((3 * F, 12 * F), bf16), V((2 * F, 3 * F), bf16), V((2, F, 3 * F), bf16),
        V((NQ, 2, 2, F, W), f32), V((NQ, 2, 6 * F, W), bf16), V((NQ, F, W), f32), V((NQ, F, W), f32),
        V((NQ, F, W), f32), V((NQ, F, W), f32), V((NQ, RING, F, W), f32), V((NQ, F, W), f32),
        V((NQ, F, W), f32), V((NQ, 2, F, W), f32), V((NQ, F, W), f32), V((NQ, F, W), f32),
        V((NP, 2, 2, F, W), f32), V((NP, 2, 2 * F, W), f32), V((NP, 2, UNK, W), f32),
        D((5,)), D((NP,)), D((NQ, 2)), D((NQ, 2)), D((NQ,)), D((NQ,)), D((NQ, 3)), D((NQ, RING)),
        D((NQ,)), D((NQ,)), D((NQ,)), D((NQ,)), D, D, D((3,)), D((RING,)),
    ]
    any_spec = pl.BlockSpec(memory_space=pl.ANY)
    return pl.pallas_call(
        kernel,
        out_shape=jax.ShapeDtypeStruct((NP, 2, UNK, W), f32),
        in_specs=[any_spec] * 6,
        out_specs=any_spec,
        scratch_shapes=scratch,
        compiler_params=pltpu.CompilerParams(
            collective_id=0, has_side_effects=True, vmem_limit_bytes=60 * 1024 * 1024
        ),
    )(*args)


def write_out(panels, out, buf, load_sem, out_sem):
    loads = [pltpu.make_async_copy(panels.at[c], buf.at[c], load_sem.at[c]) for c in range(NP)]
    stores = [
        pltpu.make_async_copy(buf.at[c], out.at[:, :, 0, pl.ds(c * W, W)], out_sem.at[c])
        for c in range(NP)
    ]
    for c in loads:
        c.start()
    for n in range(NP):
        loads[n].wait()
        stores[n].start()
    for c in stores:
        c.wait()


def in_place(panels):
    any_spec = pl.BlockSpec(memory_space=pl.ANY)
    sems = pltpu.SemaphoreType.DMA((NP,))
    return pl.pallas_call(
        write_out,
        out_shape=jax.ShapeDtypeStruct((2, UNK, 1, 512), f32),
        in_specs=[any_spec],
        out_specs=any_spec,
        scratch_shapes=[pltpu.VMEM((NP, 2, UNK, W), f32), sems, sems],
        compiler_params=pltpu.CompilerParams(vmem_limit_bytes=60 * 1024 * 1024),
    )(panels)


def per_device(right_side, start_field, block_inverse, upwind_block, south_block, north_block):
    def rows_first(a):
        return jnp.transpose(a, (0, 2, 1, 3))

    grid = rows_first(start_field).reshape(2, VARS * NODE, NODE, NODE, 1, 512)
    rest = [rows_first(a) for a in (block_inverse, south_block, north_block, upwind_block, right_side)]
    return rows_first(in_place(solve(grid, *rest)))


def solution(mesh):
    spec = P("sweep", "span", None, None)
    return jax.shard_map(
        per_device, mesh=mesh, in_specs=(spec,) * 6, out_specs=spec, check_vma=False
    )
```

```python
import jax
import jax.numpy as jnp
from jax import lax
from jax.experimental import pallas as pl
from jax.experimental.pallas import tpu as pltpu
from jax.sharding import PartitionSpec as P

VARS = 5
NODE = 5
UNK = 625
FACE = 125
F = 128
U = 640
W = 128
NP = 4
NQ = 2 * NP
RING = 4
MESH = pl.DeviceIdType.MESH
f32 = jnp.float32
bf16 = jnp.bfloat16


def dot(a, b):
    return jnp.dot(a, b, preferred_element_type=f32)


def halves(x):
    hi = x.astype(bf16)
    lo = (x - hi.astype(f32)).astype(bf16)
    return hi, lo


def left3(x):
    hi, lo = halves(x)
    return jnp.concatenate([hi, lo, hi], axis=1)


def right3(x):
    hi, lo = halves(x)
    return jnp.concatenate([hi, hi, lo], axis=0)


def product(a, b):
    return dot(left3(a), right3(b))


def kernel(
    start, b_in, s_in, n_in, u_in, f_in,
    out,
    bst, sust, fst, db5, sh, sl, fh, fl, dbst, hbst, bch, bcl, bfp, bsn3, bu3, hsn3, hu3, hlf, snr,
    gsn3, dsn3, m3, gf, g0f, phi, phik, coef, ca3, e3, phi3,
    sn, xq, gown, gpar, g0c, g0v, ag, xs, xb, tp, tin, ts, zs, hb, ob,
    load_sem, out_sem, zsend, zrecv, gsend, grecv, asend, arecv, xsend, xrecv, tsend, trecv,
    psend, precv, ksend, krecv,
):
    p = lax.axis_index("sweep")
    j = lax.axis_index("span")
    span = 16
    core = lax.rem(p, 2)
    chip = p // 2
    y = lax.rem(chip, RING)
    x = chip // RING
    mate = p + 1 - 2 * core
    up = lax.rem(j + 1, span)
    down = lax.rem(j + span - 1, span)

    def ring_peer(d):
        return (x * RING + lax.rem(y + d, RING)) * 2 + core

    over = lax.rem(p + 8, 16)

    def load(src, dst, n):
        return pltpu.make_async_copy(src, dst, load_sem.at[n])

    barrier = pltpu.get_barrier_semaphore()
    for dev in ({"span": up}, {"span": down}, {"sweep": mate}, {"sweep": over},
                {"sweep": ring_peer(1)}, {"sweep": ring_peer(2)}, {"sweep": ring_peer(3)}):
        pl.semaphore_signal(barrier, inc=1, device_id=dev, device_id_type=MESH)
    pl.semaphore_wait(barrier, 7)

    def remote(src, dst, ss, rs, dev):
        return pltpu.make_async_remote_copy(
            src_ref=src, dst_ref=dst, send_sem=ss, recv_sem=rs, device_id=dev, device_id_type=MESH
        )

    def zdev(way):
        return {"span": up if way == 0 else down}

    def zcopy1(c, way):
        level = NODE - 1 if way == 0 else 0
        src = start.at[:, :, level, :, 0, pl.ds(pl.multiple_of(c * W, W), W)]
        return remote(src, snr.at[c, way], zsend.at[c, way], zrecv.at[c, way], zdev(way))

    def zcopy2(q, way):
        c = lax.rem(q, NP)
        return remote(zs.at[c, way], sn.at[q, way], zsend.at[q, way], zrecv.at[q, way], zdev(way))

    for c in range(NP):
        for way in range(2):
            zcopy1(c, way).start()
    def gcopy(q):
        return remote(gown.at[q], gpar.at[q], gsend.at[q], grecv.at[q], {"sweep": mate})

    def acopy(q, d):
        return remote(ag.at[q, y], ag.at[q, y], asend.at[q, d - 1], arecv.at[q, y], {"sweep": ring_peer(d)})

    def aland(q, d):
        k = lax.rem(y + RING - d, RING)
        return remote(ag.at[q, k], ag.at[q, k], asend.at[q, d - 1], arecv.at[q, k], {"sweep": ring_peer(d)})

    def xcopy(q):
        return remote(xs.at[q], xb.at[q], xsend.at[q], xrecv.at[q], {"sweep": over})

    def tcopy(q):
        return remote(ts.at[q], tin.at[q], tsend.at[q], trecv.at[q], {"sweep": mate})

    def pcopy():
        return remote(phi.at[core], phi.at[core], psend, precv, {"sweep": mate})

    def kcopy(d):
        return remote(phik.at[y], phik.at[y], ksend.at[d - 1], krecv.at[y], {"sweep": ring_peer(d)})

    def kland(d):
        k = lax.rem(y + RING - d, RING)
        return remote(phik.at[k], phik.at[k], ksend.at[d - 1], krecv.at[k], {"sweep": ring_peer(d)})

    b_load = load(b_in.at[:, :, 0, :], bst, 0)
    d_loads = [
        load(b_in.at[:, pl.ds(125 * v + 100, 25), 0, :], db5.at[v], 5 + v) for v in range(VARS)
    ]
    for c in d_loads:
        c.start()
    su_loads = [load(m.at[:, :, 0, :], sust.at[n], 1 + n) for n, m in enumerate((s_in, n_in, u_in))]
    for c in su_loads:
        c.start()
    f_load = load(f_in.at[:, :, 0, :], fst, 4)
    f_load.start()

    edge = pl.ds(U - F, F)
    hbst[:, edge] = jnp.zeros((2 * F, F), f32)
    hbst[FACE:F, :] = jnp.zeros((F - FACE, U), f32)
    hbst[F + FACE:, :] = jnp.zeros((F - FACE, U), f32)
    bch[:, edge] = jnp.zeros((160, F), bf16)
    bcl[:, edge] = jnp.zeros((160, F), bf16)
    for e in range(2):
        dbst[e, :, edge] = jnp.zeros((F, F), f32)
        dbst[e, FACE:, :] = jnp.zeros((F - FACE, U), f32)
        for ref in (sh, sl):
            ref[e] = jnp.zeros((U, 3 * F), bf16)
        for ref in (fh, fl):
            ref[e, U - 16:, :] = jnp.zeros((16, 512), bf16)

    for v in range(VARS):
        d_loads[v].wait()
        for e in range(2):
            dbst[e, 25 * v:25 * v + 25, :UNK] = db5[v, e]
    for n in range(3):
        su_loads[n].wait()
        for e in range(2):
            hi, lo = halves(sust[n, e])
            sh[e, :UNK, F * n:F * n + FACE] = hi
            sl[e, :UNK, F * n:F * n + FACE] = lo
    b_load.start()
    dsnu = []
    dbs = []
    for e in range(2):
        hi, lo = halves(dbst[e])
        dbs.append((hi, lo))
        dsnu.append(dot(hi, sh[e]) + dot(hi, sl[e]) + dot(lo, sh[e]))
    m0 = dsnu[0][:, 2 * F:]
    m1 = dsnu[1][:, 2 * F:]
    m3[0] = left3(m0)
    m3[1] = left3(m1)
    dsn3[...] = left3(dsnu[0][:, :2 * F])
    gsn3[:, :6 * F] = left3(-dot(m3[1], right3(dsnu[0][:, :2 * F])))
    gsn3[:, 6 * F:] = left3(dsnu[1][:, :2 * F])
    phi[core] = dot(m3[1], right3(m0))
    pcopy().start()
    f_load.wait()
    for e in range(2):
        hi, lo = halves(fst[e])
        fh[e, :UNK, :] = hi
        fl[e, :UNK, :] = lo
    df = []
    for e in range(2):
        hi, lo = dbs[e]
        df.append(dot(hi, fh[e]) + dot(hi, fl[e]) + dot(lo, fh[e]))
    gall = df[1] - dot(m3[1], right3(df[0]))
    for c in range(NP):
        g0f[c] = df[0][:, W * c:W * c + W]
        gf[c] = gall[:, W * c:W * c + W]
    pcopy().wait_recv()
    phi3[0] = left3(phi[0])
    phi3[1] = left3(phi[1])
    phik[y] = dot(phi3[1], right3(phi[0]))
    for d in (1, 2, 3):
        kcopy(d).start()

    def chunks_by(k):
        return jnp.clip(k - 5, 0, 2) + 2 * jnp.clip(k - 7, 0, 3)

    def blocks(first, last):
        def one(n, _):
            e = n // 4
            m = lax.rem(n, 4)
            rows = pl.ds(pl.multiple_of(m * 160, 160), 160)

            @pl.when(m < 3)
            def _():
                hi, lo = halves(bst[e, rows, :])
                bch[:, :UNK] = hi
                bcl[:, :UNK] = lo

            @pl.when(m == 3)
            def _():
                hi, lo = halves(bst[e, 480:UNK, :])
                bch[:UNK - 480, :UNK] = hi
                bcl[:UNK - 480, :UNK] = lo

            hi = bch[...]
            lo = bcl[...]
            r = dot(hi, sh[e]) + dot(hi, sl[e]) + dot(lo, sh[e])
            bsn3[e, rows, :] = left3(r[:, :2 * F])
            bu3[e, rows, :] = left3(r[:, 2 * F:])
            r = dot(hi, fh[e]) + dot(hi, fl[e]) + dot(lo, fh[e])
            for c in range(NP):
                bfp[c, e, rows, :] = r[:, W * c:W * c + W]
            return 0

        lax.fori_loop(first, last, one, 0)

    def face_rows(e):
        for g in range(25):
            hbst[5 * g:5 * g + 5, :UNK] = bst[e, 25 * g + 20:25 * g + 25, :]
            hbst[F + 5 * g:F + 5 * g + 5, :UNK] = bst[e, 25 * g:25 * g + 5, :]
        hi, lo = halves(hbst[...])
        r = dot(hi, sh[e]) + dot(hi, sl[e]) + dot(lo, sh[e])
        hsn3[e] = left3(r[:, :2 * F])
        hu3[e] = left3(r[:, 2 * F:])
        r = dot(hi, fh[e]) + dot(hi, fl[e]) + dot(lo, fh[e])
        for c in range(NP):
            hlf[c, e] = r[:, W * c:W * c + W]

    def coefficients():
        for d in (1, 2, 3):
            kland(d).wait_recv()
        eye = (lax.broadcasted_iota(jnp.int32, (F, F), 0) == lax.broadcasted_iota(jnp.int32, (F, F), 1)).astype(f32)
        coef[0] = eye
        coef[1] = eye

        def one(n, _):
            k = RING - 1 - n
            r = coef[0]
            s = coef[1]
            zero = jnp.zeros((F, F), f32)
            before = k < y
            a = jnp.where(before, r, zero)
            both = dot(left3(jnp.concatenate([r, s], axis=0)), right3(phik[k]))
            coef[0] = jnp.where(before, both[:F], r)
            coef[1] = both[F:]
            ua = dot(phi3[0], right3(a))
            col = pl.ds(pl.multiple_of(k * 3 * F, 3 * F), 3 * F)
            ca3[:, col] = left3(jnp.concatenate([a, ua, s], axis=0))
            return 0

        lax.fori_loop(0, RING, one, 0)
        e_map = coef[0]
        e3[:F, :] = left3(e_map)
        e3[F:, :] = left3(dot(phi3[0], right3(e_map)))

    def trace_in(q, c, lead):
        @pl.when(q < NP)
        def _():
            for way in range(2):
                zcopy1(c, way).wait_recv()
                for e in range(2):
                    sn[q, way, e, FACE:, :] = jnp.zeros((F - FACE, W), f32)
                    for g in range(25):
                        sn[q, way, e, 5 * g:5 * g + 5, :] = snr[c, way, e, g]

        @pl.when(q >= NP)
        def _():
            for way in range(2):
                zcopy2(q, way).wait_recv()

        for e in range(2):
            xq[q, e] = right3(jnp.concatenate([sn[q, 0, e], sn[q, 1, e]], axis=0))
        x0 = xq[q, 0]
        gown[q] = gf[c] - dot(gsn3[...], jnp.concatenate([x0, xq[q, 1]], axis=0))

        @pl.when(jnp.logical_not(lead))
        def _():
            gcopy(q).start()

        g0v[q] = g0f[c] - dot(dsn3[...], x0)

    def pair_up(q, c, lead):
        @pl.when(lead)
        def _():
            gcopy(q).wait_recv()
            own = gown[q]
            other = gpar[q]
            first = jnp.where(core == 0, own, other)
            second = jnp.where(core == 0, other, own)
            g0c[q] = first
            ag[q, y] = second + dot(phi3[1], right3(first))
            for d in (2, 1, 3):
                acopy(q, d).start()

    def settle(q, here, after):
        tin[q] = jnp.where(core == 0, here, after)
        ts[q] = jnp.where(core == 0, after, here)
        tcopy(q).start()

    def ring_sum(q, c, lead):
        @pl.when(lead)
        def _():
            for d in (1, 2, 3):
                aland(q, d).wait_recv()
            stack = jnp.concatenate([right3(ag[q, k]) for k in range(RING)], axis=0)
            r = dot(ca3[...], stack)

            @pl.when(x == 0)
            def _():
                xs[q] = r[2 * F:]
                xcopy(q).start()
                settle(q, r[:F], r[F:2 * F] + g0c[q])

            @pl.when(x == 1)
            def _():
                tp[q, 0] = r[:F]
                tp[q, 1] = r[F:2 * F] + g0c[q]

    def cross(q, c, lead):
        @pl.when(jnp.logical_and(lead, x == 1))
        def _():
            xcopy(q).wait_recv()
            r = dot(e3[...], right3(xb[q]))
            settle(q, tp[q, 0] + r[:F], tp[q, 1] + r[F:])

    def base1(q, c, lead):
        @pl.when(q < NP)
        def _():
            for e in range(2):
                hb[c, e] = hlf[c, e] - dot(hsn3[e], xq[q, e])

    def base2(q, c, lead):
        @pl.when(q >= NP)
        def _():
            for e in range(2):
                ob[c, e] = bfp[c, e, :UNK, :] - dot(bsn3[e], xq[q, e])[:UNK]

    def out_copy(c):
        return pltpu.make_async_copy(
            ob.at[c], out.at[c], out_sem.at[c]
        )

    def finish(q, c, lead):
        @pl.when(jnp.logical_not(lead))
        def _():
            tcopy(q).wait_recv()

        t0 = right3(tin[q])
        t1 = right3(g0v[q] - dot(m3[0], t0))

        @pl.when(q < NP)
        def _():
            for e, t in ((0, t0), (1, t1)):
                h = hb[c, e] - dot(hu3[e], t)
                zs[c, 0, e] = h[:F]
                zs[c, 1, e] = h[F:]
            for way in range(2):
                zcopy2(q + NP, way).start()

        @pl.when(q >= NP)
        def _():
            for e, t in ((0, t0), (1, t1)):
                ob[c, e] = ob[c, e] - dot(bu3[e], t)[:UNK]
            out_copy(c).start()

    gap = 7

    def slot(k, _):
        def at(behind, stage):
            n = k - behind
            active = jnp.logical_or(
                jnp.logical_and(n >= 0, n < NP), jnp.logical_and(n >= gap, n < gap + NP)
            )

            @pl.when(active)
            def _():
                late = (n >= gap).astype(jnp.int32)
                c = n - gap * late
                q = c + NP * late
                stage(q, c, core == lax.rem(c, 2))

        at(5, finish)
        at(4, cross)
        at(4, base1)
        at(3, ring_sum)
        at(3, base2)
        at(1, pair_up)
        at(0, trace_in)
        @pl.when(k == 1)
        def _():
            coefficients()

        @pl.when(k == 0)
        def _():
            b_load.wait()

        @pl.when(k < 2)
        def _():
            face_rows(k)

        @pl.when(jnp.logical_and(k >= 5, k < 10))
        def _():
            blocks(chunks_by(k), chunks_by(k + 1))


        return 0

    lax.fori_loop(0, gap + NP + 5, slot, 0)

    pcopy().wait_send()
    for c in range(NP):
        for way in range(2):
            zcopy1(c, way).wait_send()
            zcopy2(c + NP, way).wait_send()
    for d in (1, 2, 3):
        kcopy(d).wait_send()

    def drain(q, _):
        lead = core == lax.rem(q, 2)

        @pl.when(lead)
        def _():
            for d in (1, 2, 3):
                acopy(q, d).wait_send()
            tcopy(q).wait_send()

            @pl.when(x == 0)
            def _():
                xcopy(q).wait_send()

        @pl.when(jnp.logical_not(lead))
        def _():
            gcopy(q).wait_send()

        return 0

    lax.fori_loop(0, NQ, drain, 0)
    for c in range(NP):
        out_copy(c).wait()


def solve(*args):
    V = pltpu.VMEM
    D = pltpu.SemaphoreType.DMA
    scratch = [
        V((2, UNK, UNK), f32), V((3, 2, UNK, FACE), f32), V((2, UNK, 512), f32),
        V((VARS, 2, 25, UNK), f32),
        V((2, U, 3 * F), bf16), V((2, U, 3 * F), bf16), V((2, U, 512), bf16), V((2, U, 512), bf16),
        V((2, F, U), f32), V((2 * F, U), f32), V((160, U), bf16), V((160, U), bf16),
        V((NP, 2, U, W), f32), V((2, U, 6 * F), bf16), V((2, U, 3 * F), bf16),
        V((2, 2 * F, 6 * F), bf16), V((2, 2 * F, 3 * F), bf16), V((NP, 2, 2 * F, W), f32),
        V((NP, 2, 2, 25, NODE, W), f32),
        V((F, 12 * F), bf16), V((F, 6 * F), bf16), V((2, F, 3 * F), bf16), V((NP, F, W), f32),
        V((NP, F, W), f32), V((2, F, F), f32), V((RING, F, F), f32), V((2, F, F), f32),
        V((3 * F, 12 * F), bf16), V((2 * F, 3 * F), bf16), V((2, F, 3 * F), bf16),
        V((NQ, 2, 2, F, W), f32), V((NQ, 2, 6 * F, W), bf16), V((NQ, F, W), f32), V((NQ, F, W), f32),
        V((NQ, F, W), f32), V((NQ, F, W), f32), V((NQ, RING, F, W), f32), V((NQ, F, W), f32),
        V((NQ, F, W), f32), V((NQ, 2, F, W), f32), V((NQ, F, W), f32), V((NQ, F, W), f32),
        V((NP, 2, 2, F, W), f32), V((NP, 2, 2 * F, W), f32), V((NP, 2, UNK, W), f32),
        D((10,)), D((NP,)), D((NQ, 2)), D((NQ, 2)), D((NQ,)), D((NQ,)), D((NQ, 3)), D((NQ, RING)),
        D((NQ,)), D((NQ,)), D((NQ,)), D((NQ,)), D, D, D((3,)), D((RING,)),
    ]
    any_spec = pl.BlockSpec(memory_space=pl.ANY)
    return pl.pallas_call(
        kernel,
        out_shape=jax.ShapeDtypeStruct((NP, 2, UNK, W), f32),
        in_specs=[any_spec] * 6,
        out_specs=any_spec,
        scratch_shapes=scratch,
        compiler_params=pltpu.CompilerParams(
            collective_id=0, has_side_effects=True, vmem_limit_bytes=60 * 1024 * 1024
        ),
    )(*args)


def write_out(panels, out, buf, load_sem, out_sem):
    pieces = [(c, e) for c in range(NP) for e in range(2)]
    loads = [
        pltpu.make_async_copy(panels.at[c, e], buf.at[c, e], load_sem.at[c, e]) for c, e in pieces
    ]
    stores = [
        pltpu.make_async_copy(
            buf.at[c, e], out.at[e, :, 0, pl.ds(c * W, W)], out_sem.at[c, e]
        )
        for c, e in pieces
    ]
    for c in loads:
        c.start()
    for a, b in zip(loads, stores):
        a.wait()
        b.start()
    for c in stores:
        c.wait()


def in_place(panels):
    any_spec = pl.BlockSpec(memory_space=pl.ANY)
    sems = pltpu.SemaphoreType.DMA((NP, 2))
    return pl.pallas_call(
        write_out,
        out_shape=jax.ShapeDtypeStruct((2, UNK, 1, 512), f32),
        in_specs=[any_spec],
        out_specs=any_spec,
        scratch_shapes=[pltpu.VMEM((NP, 2, UNK, W), f32), sems, sems],
        compiler_params=pltpu.CompilerParams(vmem_limit_bytes=60 * 1024 * 1024),
    )(panels)


def per_device(right_side, start_field, block_inverse, upwind_block, south_block, north_block):
    def rows_first(a):
        return jnp.transpose(a, (0, 2, 1, 3))

    grid = rows_first(start_field).reshape(2, VARS * NODE, NODE, NODE, 1, 512)
    rest = [rows_first(a) for a in (block_inverse, south_block, north_block, upwind_block, right_side)]
    return rows_first(in_place(solve(grid, *rest)))


def solution(mesh):
    spec = P("sweep", "span", None, None)
    return jax.shard_map(
        per_device, mesh=mesh, in_specs=(spec,) * 6, out_specs=spec, check_vma=False
    )
```

```python
import jax
import jax.numpy as jnp
from jax import lax
from jax.experimental import pallas as pl
from jax.experimental.pallas import tpu as pltpu
from jax.sharding import PartitionSpec as P

VARS = 5
NODE = 5
UNK = 625
FACE = 125
F = 128
U = 640
W = 128
NP = 4
NQ = 2 * NP
RING = 4
MESH = pl.DeviceIdType.MESH
f32 = jnp.float32
bf16 = jnp.bfloat16


def dot(a, b):
    return jnp.dot(a, b, preferred_element_type=f32)


def halves(x):
    hi = x.astype(bf16)
    lo = (x - hi.astype(f32)).astype(bf16)
    return hi, lo


def left3(x):
    hi, lo = halves(x)
    return jnp.concatenate([hi, lo, hi], axis=1)


def right3(x):
    hi, lo = halves(x)
    return jnp.concatenate([hi, hi, lo], axis=0)


def product(a, b):
    return dot(left3(a), right3(b))


def kernel(
    start, b_in, s_in, n_in, u_in, f_in,
    out,
    bst, sust, fst, db5, sh, sl, fh, fl, dbst, hbst, bch, bcl, bfp, bsn3, bu3, hsn3, hu3, hlf, snr,
    gsn3, dsn3, m3, gf, g0f, phi, phik, coef, ca3, e3, phi3,
    sn, xq, gown, gpar, g0c, g0v, ag, xs, xb, tp, tin, ts, zs, hb, ob,
    load_sem, out_sem, zsend, zrecv, gsend, grecv, asend, arecv, xsend, xrecv, tsend, trecv,
    psend, precv, ksend, krecv,
):
    p = lax.axis_index("sweep")
    j = lax.axis_index("span")
    span = 16
    core = lax.rem(p, 2)
    chip = p // 2
    y = lax.rem(chip, RING)
    x = chip // RING
    mate = p + 1 - 2 * core
    up = lax.rem(j + 1, span)
    down = lax.rem(j + span - 1, span)

    def ring_peer(d):
        return (x * RING + lax.rem(y + d, RING)) * 2 + core

    over = lax.rem(p + 8, 16)

    def load(src, dst, n):
        return pltpu.make_async_copy(src, dst, load_sem.at[n])

    barrier = pltpu.get_barrier_semaphore()
    for dev in ({"span": up}, {"span": down}, {"sweep": mate}, {"sweep": over},
                {"sweep": ring_peer(1)}, {"sweep": ring_peer(2)}, {"sweep": ring_peer(3)}):
        pl.semaphore_signal(barrier, inc=1, device_id=dev, device_id_type=MESH)

    b_load = load(b_in.at[:, :, 0, :], bst, 0)
    d_loads = [
        load(b_in.at[:, pl.ds(125 * v + 100, 25), 0, :], db5.at[v], 5 + v) for v in range(VARS)
    ]
    for c in d_loads:
        c.start()
    su_loads = [load(m.at[:, :, 0, :], sust.at[n], 1 + n) for n, m in enumerate((s_in, n_in, u_in))]
    for c in su_loads:
        c.start()
    f_load = load(f_in.at[:, :, 0, :], fst, 4)
    f_load.start()

    pl.semaphore_wait(barrier, 7)

    def remote(src, dst, ss, rs, dev):
        return pltpu.make_async_remote_copy(
            src_ref=src, dst_ref=dst, send_sem=ss, recv_sem=rs, device_id=dev, device_id_type=MESH
        )

    def zdev(way):
        return {"span": up if way == 0 else down}

    def zcopy1(c, way):
        level = NODE - 1 if way == 0 else 0
        src = start.at[:, :, level, :, 0, pl.ds(pl.multiple_of(c * W, W), W)]
        return remote(src, snr.at[c, way], zsend.at[c, way], zrecv.at[c, way], zdev(way))

    def zcopy2(q, way):
        c = lax.rem(q, NP)
        return remote(zs.at[c, way], sn.at[q, way], zsend.at[q, way], zrecv.at[q, way], zdev(way))

    for c in range(NP):
        for way in range(2):
            zcopy1(c, way).start()
    def gcopy(q):
        return remote(gown.at[q], gpar.at[q], gsend.at[q], grecv.at[q], {"sweep": mate})

    def acopy(q, d):
        return remote(ag.at[q, y], ag.at[q, y], asend.at[q, d - 1], arecv.at[q, y], {"sweep": ring_peer(d)})

    def aland(q, d):
        k = lax.rem(y + RING - d, RING)
        return remote(ag.at[q, k], ag.at[q, k], asend.at[q, d - 1], arecv.at[q, k], {"sweep": ring_peer(d)})

    def xcopy(q):
        return remote(xs.at[q], xb.at[q], xsend.at[q], xrecv.at[q], {"sweep": over})

    def tcopy(q):
        return remote(ts.at[q], tin.at[q], tsend.at[q], trecv.at[q], {"sweep": mate})

    def pcopy():
        return remote(phi.at[core], phi.at[core], psend, precv, {"sweep": mate})

    def kcopy(d):
        return remote(phik.at[y], phik.at[y], ksend.at[d - 1], krecv.at[y], {"sweep": ring_peer(d)})

    def kland(d):
        k = lax.rem(y + RING - d, RING)
        return remote(phik.at[k], phik.at[k], ksend.at[d - 1], krecv.at[k], {"sweep": ring_peer(d)})

    edge = pl.ds(U - F, F)
    hbst[:, edge] = jnp.zeros((2 * F, F), f32)
    hbst[FACE:F, :] = jnp.zeros((F - FACE, U), f32)
    hbst[F + FACE:, :] = jnp.zeros((F - FACE, U), f32)
    bch[:, edge] = jnp.zeros((160, F), bf16)
    bcl[:, edge] = jnp.zeros((160, F), bf16)
    for e in range(2):
        dbst[e, :, edge] = jnp.zeros((F, F), f32)
        dbst[e, FACE:, :] = jnp.zeros((F - FACE, U), f32)
        for ref in (sh, sl):
            ref[e] = jnp.zeros((U, 3 * F), bf16)
        for ref in (fh, fl):
            ref[e, U - 16:, :] = jnp.zeros((16, 512), bf16)

    for v in range(VARS):
        d_loads[v].wait()
        for e in range(2):
            dbst[e, 25 * v:25 * v + 25, :UNK] = db5[v, e]
    for n in range(3):
        su_loads[n].wait()
        for e in range(2):
            hi, lo = halves(sust[n, e])
            sh[e, :UNK, F * n:F * n + FACE] = hi
            sl[e, :UNK, F * n:F * n + FACE] = lo
    b_load.start()
    dsnu = []
    dbs = []
    for e in range(2):
        hi, lo = halves(dbst[e])
        dbs.append((hi, lo))
        dsnu.append(dot(hi, sh[e]) + dot(hi, sl[e]) + dot(lo, sh[e]))
    m0 = dsnu[0][:, 2 * F:]
    m1 = dsnu[1][:, 2 * F:]
    m3[0] = left3(m0)
    m3[1] = left3(m1)
    dsn3[...] = left3(dsnu[0][:, :2 * F])
    gsn3[:, :6 * F] = left3(-dot(m3[1], right3(dsnu[0][:, :2 * F])))
    gsn3[:, 6 * F:] = left3(dsnu[1][:, :2 * F])
    phi[core] = dot(m3[1], right3(m0))
    pcopy().start()
    f_load.wait()
    for e in range(2):
        hi, lo = halves(fst[e])
        fh[e, :UNK, :] = hi
        fl[e, :UNK, :] = lo
    df = []
    for e in range(2):
        hi, lo = dbs[e]
        df.append(dot(hi, fh[e]) + dot(hi, fl[e]) + dot(lo, fh[e]))
    gall = df[1] - dot(m3[1], right3(df[0]))
    for c in range(NP):
        g0f[c] = df[0][:, W * c:W * c + W]
        gf[c] = gall[:, W * c:W * c + W]
    pcopy().wait_recv()
    phi3[0] = left3(phi[0])
    phi3[1] = left3(phi[1])
    phik[y] = dot(phi3[1], right3(phi[0]))
    for d in (1, 2, 3):
        kcopy(d).start()

    def chunks_by(k):
        return jnp.clip(k - 5, 0, 2) + 2 * jnp.clip(k - 7, 0, 3)

    def blocks(first, last):
        def one(n, _):
            e = n // 4
            m = lax.rem(n, 4)
            rows = pl.ds(pl.multiple_of(m * 160, 160), 160)

            @pl.when(m < 3)
            def _():
                hi, lo = halves(bst[e, rows, :])
                bch[:, :UNK] = hi
                bcl[:, :UNK] = lo

            @pl.when(m == 3)
            def _():
                hi, lo = halves(bst[e, 480:UNK, :])
                bch[:UNK - 480, :UNK] = hi
                bcl[:UNK - 480, :UNK] = lo

            hi = bch[...]
            lo = bcl[...]
            r = dot(hi, sh[e]) + dot(hi, sl[e]) + dot(lo, sh[e])
            bsn3[e, rows, :] = left3(r[:, :2 * F])
            bu3[e, rows, :] = left3(r[:, 2 * F:])
            r = dot(hi, fh[e]) + dot(hi, fl[e]) + dot(lo, fh[e])
            for c in range(NP):
                bfp[c, e, rows, :] = r[:, W * c:W * c + W]
            return 0

        lax.fori_loop(first, last, one, 0)

    def face_rows(e):
        for g in range(25):
            hbst[5 * g:5 * g + 5, :UNK] = bst[e, 25 * g + 20:25 * g + 25, :]
            hbst[F + 5 * g:F + 5 * g + 5, :UNK] = bst[e, 25 * g:25 * g + 5, :]
        hi, lo = halves(hbst[...])
        r = dot(hi, sh[e]) + dot(hi, sl[e]) + dot(lo, sh[e])
        hsn3[e] = left3(r[:, :2 * F])
        hu3[e] = left3(r[:, 2 * F:])
        r = dot(hi, fh[e]) + dot(hi, fl[e]) + dot(lo, fh[e])
        for c in range(NP):
            hlf[c, e] = r[:, W * c:W * c + W]

    def coefficients():
        for d in (1, 2, 3):
            kland(d).wait_recv()
        eye = (lax.broadcasted_iota(jnp.int32, (F, F), 0) == lax.broadcasted_iota(jnp.int32, (F, F), 1)).astype(f32)
        coef[0] = eye
        coef[1] = eye

        def one(n, _):
            k = RING - 1 - n
            r = coef[0]
            s = coef[1]
            zero = jnp.zeros((F, F), f32)
            before = k < y
            a = jnp.where(before, r, zero)
            both = dot(left3(jnp.concatenate([r, s], axis=0)), right3(phik[k]))
            coef[0] = jnp.where(before, both[:F], r)
            coef[1] = both[F:]
            ua = dot(phi3[0], right3(a))
            col = pl.ds(pl.multiple_of(k * 3 * F, 3 * F), 3 * F)
            ca3[:, col] = left3(jnp.concatenate([a, ua, s], axis=0))
            return 0

        lax.fori_loop(0, RING, one, 0)
        e_map = coef[0]
        e3[:F, :] = left3(e_map)
        e3[F:, :] = left3(dot(phi3[0], right3(e_map)))

    def trace_in(q, c, lead):
        @pl.when(q < NP)
        def _():
            for way in range(2):
                zcopy1(c, way).wait_recv()
                for e in range(2):
                    sn[q, way, e, FACE:, :] = jnp.zeros((F - FACE, W), f32)
                    for g in range(25):
                        sn[q, way, e, 5 * g:5 * g + 5, :] = snr[c, way, e, g]

        @pl.when(q >= NP)
        def _():
            for way in range(2):
                zcopy2(q, way).wait_recv()

        for e in range(2):
            xq[q, e] = right3(jnp.concatenate([sn[q, 0, e], sn[q, 1, e]], axis=0))
        x0 = xq[q, 0]
        gown[q] = gf[c] - dot(gsn3[...], jnp.concatenate([x0, xq[q, 1]], axis=0))

        @pl.when(jnp.logical_not(lead))
        def _():
            gcopy(q).start()

        g0v[q] = g0f[c] - dot(dsn3[...], x0)

    def pair_up(q, c, lead):
        @pl.when(lead)
        def _():
            gcopy(q).wait_recv()
            own = gown[q]
            other = gpar[q]
            first = jnp.where(core == 0, own, other)
            second = jnp.where(core == 0, other, own)
            g0c[q] = first
            ag[q, y] = second + dot(phi3[1], right3(first))
            for d in (2, 1, 3):
                acopy(q, d).start()

    def settle(q, here, after):
        tin[q] = jnp.where(core == 0, here, after)
        ts[q] = jnp.where(core == 0, after, here)
        tcopy(q).start()

    def ring_sum(q, c, lead):
        @pl.when(lead)
        def _():
            for d in (1, 2, 3):
                aland(q, d).wait_recv()
            stack = jnp.concatenate([right3(ag[q, k]) for k in range(RING)], axis=0)
            r = dot(ca3[...], stack)

            @pl.when(x == 0)
            def _():
                xs[q] = r[2 * F:]
                xcopy(q).start()
                settle(q, r[:F], r[F:2 * F] + g0c[q])

            @pl.when(x == 1)
            def _():
                tp[q, 0] = r[:F]
                tp[q, 1] = r[F:2 * F] + g0c[q]

    def cross(q, c, lead):
        @pl.when(jnp.logical_and(lead, x == 1))
        def _():
            xcopy(q).wait_recv()
            r = dot(e3[...], right3(xb[q]))
            settle(q, tp[q, 0] + r[:F], tp[q, 1] + r[F:])

    def base1(q, c, lead):
        @pl.when(q < NP)
        def _():
            for e in range(2):
                hb[c, e] = hlf[c, e] - dot(hsn3[e], xq[q, e])

    def base2(q, c, lead):
        @pl.when(q >= NP)
        def _():
            for e in range(2):
                ob[c, e] = bfp[c, e, :UNK, :] - dot(bsn3[e], xq[q, e])[:UNK]

    def out_copy(c):
        return pltpu.make_async_copy(
            ob.at[c], out.at[c], out_sem.at[c]
        )

    def finish(q, c, lead):
        @pl.when(jnp.logical_not(lead))
        def _():
            tcopy(q).wait_recv()

        t0 = right3(tin[q])
        t1 = right3(g0v[q] - dot(m3[0], t0))

        @pl.when(q < NP)
        def _():
            for e, t in ((0, t0), (1, t1)):
                h = hb[c, e] - dot(hu3[e], t)
                zs[c, 0, e] = h[:F]
                zs[c, 1, e] = h[F:]
            for way in range(2):
                zcopy2(q + NP, way).start()

        @pl.when(q >= NP)
        def _():
            for e, t in ((0, t0), (1, t1)):
                ob[c, e] = ob[c, e] - dot(bu3[e], t)[:UNK]
            out_copy(c).start()

    gap = 7

    def slot(k, _):
        def at(behind, stage):
            n = k - behind
            active = jnp.logical_or(
                jnp.logical_and(n >= 0, n < NP), jnp.logical_and(n >= gap, n < gap + NP)
            )

            @pl.when(active)
            def _():
                late = (n >= gap).astype(jnp.int32)
                c = n - gap * late
                q = c + NP * late
                stage(q, c, core == lax.rem(c, 2))

        at(5, finish)
        at(4, cross)
        at(4, base1)
        at(3, ring_sum)
        at(3, base2)
        at(1, pair_up)
        at(0, trace_in)
        @pl.when(k == 1)
        def _():
            coefficients()

        @pl.when(k == 0)
        def _():
            b_load.wait()

        @pl.when(k < 2)
        def _():
            face_rows(k)

        @pl.when(jnp.logical_and(k >= 5, k < 10))
        def _():
            blocks(chunks_by(k), chunks_by(k + 1))


        return 0

    lax.fori_loop(0, gap + NP + 5, slot, 0)

    pcopy().wait_send()
    for c in range(NP):
        for way in range(2):
            zcopy1(c, way).wait_send()
            zcopy2(c + NP, way).wait_send()
    for d in (1, 2, 3):
        kcopy(d).wait_send()

    def drain(q, _):
        lead = core == lax.rem(q, 2)

        @pl.when(lead)
        def _():
            for d in (1, 2, 3):
                acopy(q, d).wait_send()
            tcopy(q).wait_send()

            @pl.when(x == 0)
            def _():
                xcopy(q).wait_send()

        @pl.when(jnp.logical_not(lead))
        def _():
            gcopy(q).wait_send()

        return 0

    lax.fori_loop(0, NQ, drain, 0)
    for c in range(NP):
        out_copy(c).wait()


def solve(*args):
    V = pltpu.VMEM
    D = pltpu.SemaphoreType.DMA
    scratch = [
        V((2, UNK, UNK), f32), V((3, 2, UNK, FACE), f32), V((2, UNK, 512), f32),
        V((VARS, 2, 25, UNK), f32),
        V((2, U, 3 * F), bf16), V((2, U, 3 * F), bf16), V((2, U, 512), bf16), V((2, U, 512), bf16),
        V((2, F, U), f32), V((2 * F, U), f32), V((160, U), bf16), V((160, U), bf16),
        V((NP, 2, U, W), f32), V((2, U, 6 * F), bf16), V((2, U, 3 * F), bf16),
        V((2, 2 * F, 6 * F), bf16), V((2, 2 * F, 3 * F), bf16), V((NP, 2, 2 * F, W), f32),
        V((NP, 2, 2, 25, NODE, W), f32),
        V((F, 12 * F), bf16), V((F, 6 * F), bf16), V((2, F, 3 * F), bf16), V((NP, F, W), f32),
        V((NP, F, W), f32), V((2, F, F), f32), V((RING, F, F), f32), V((2, F, F), f32),
        V((3 * F, 12 * F), bf16), V((2 * F, 3 * F), bf16), V((2, F, 3 * F), bf16),
        V((NQ, 2, 2, F, W), f32), V((NQ, 2, 6 * F, W), bf16), V((NQ, F, W), f32), V((NQ, F, W), f32),
        V((NQ, F, W), f32), V((NQ, F, W), f32), V((NQ, RING, F, W), f32), V((NQ, F, W), f32),
        V((NQ, F, W), f32), V((NQ, 2, F, W), f32), V((NQ, F, W), f32), V((NQ, F, W), f32),
        V((NP, 2, 2, F, W), f32), V((NP, 2, 2 * F, W), f32), V((NP, 2, UNK, W), f32),
        D((10,)), D((NP,)), D((NQ, 2)), D((NQ, 2)), D((NQ,)), D((NQ,)), D((NQ, 3)), D((NQ, RING)),
        D((NQ,)), D((NQ,)), D((NQ,)), D((NQ,)), D, D, D((3,)), D((RING,)),
    ]
    any_spec = pl.BlockSpec(memory_space=pl.ANY)
    return pl.pallas_call(
        kernel,
        out_shape=jax.ShapeDtypeStruct((NP, 2, UNK, W), f32),
        in_specs=[any_spec] * 6,
        out_specs=any_spec,
        scratch_shapes=scratch,
        compiler_params=pltpu.CompilerParams(
            collective_id=0, has_side_effects=True, vmem_limit_bytes=60 * 1024 * 1024
        ),
    )(*args)


def write_out(panels, out, buf, load_sem, out_sem):
    pieces = [(c, e) for c in range(NP) for e in range(2)]
    loads = [
        pltpu.make_async_copy(panels.at[c, e], buf.at[c, e], load_sem.at[c, e]) for c, e in pieces
    ]
    stores = [
        pltpu.make_async_copy(
            buf.at[c, e], out.at[e, :, 0, pl.ds(c * W, W)], out_sem.at[c, e]
        )
        for c, e in pieces
    ]
    for c in loads:
        c.start()
    for a, b in zip(loads, stores):
        a.wait()
        b.start()
    for c in stores:
        c.wait()


def in_place(panels):
    any_spec = pl.BlockSpec(memory_space=pl.ANY)
    sems = pltpu.SemaphoreType.DMA((NP, 2))
    return pl.pallas_call(
        write_out,
        out_shape=jax.ShapeDtypeStruct((2, UNK, 1, 512), f32),
        in_specs=[any_spec],
        out_specs=any_spec,
        scratch_shapes=[pltpu.VMEM((NP, 2, UNK, W), f32), sems, sems],
        compiler_params=pltpu.CompilerParams(vmem_limit_bytes=60 * 1024 * 1024),
    )(panels)


def per_device(right_side, start_field, block_inverse, upwind_block, south_block, north_block):
    def rows_first(a):
        return jnp.transpose(a, (0, 2, 1, 3))

    grid = rows_first(start_field).reshape(2, VARS * NODE, NODE, NODE, 1, 512)
    rest = [rows_first(a) for a in (block_inverse, south_block, north_block, upwind_block, right_side)]
    return rows_first(in_place(solve(grid, *rest)))


def solution(mesh):
    spec = P("sweep", "span", None, None)
    return jax.shard_map(
        per_device, mesh=mesh, in_specs=(spec,) * 6, out_specs=spec, check_vma=False
    )
```
